32 devices in a mesh: dp: 8 (over y, x, core), expert: 4 (over z).
Axes of the slice: x: 2, y: 2, z: 4, core: 2. Of those that a mesh axis runs over, the one named last changes fastest.
Arguments:
- tokens: bfloat16 [1024, 2048], P('expert'), may hold values from -6 to 6
- grad_out: bfloat16 [1024, 2048], P('expert'), may hold values from -6 to 6
- expert_ids: int32 [1024, 1], P('expert'), may hold values from 0 to 3; in each aligned block of 256 rows (0 to 255, 256 to 511, ...) at most 160 rows name the same one
- gate_prob: float32 [1024, 1], P('expert'), may hold values from 0.2 to 1
- w_gate: bfloat16 [4, 2048, 4096], P('expert', None, 'dp'), may hold values from -0.125 to 0.125
- w_up: bfloat16 [4, 2048, 4096], P('expert', None, 'dp'), may hold values from -0.125 to 0.125
- w_down: bfloat16 [4, 4096, 2048], P('expert', 'dp'), may hold values from -0.09375 to 0.09375
Outputs:
- grad_tokens: bfloat16 [1024, 2048], P('expert')
- grad_gate: bfloat16 [4, 2048, 4096], P('expert', None, 'dp')
- grad_up: bfloat16 [4, 2048, 4096], P('expert', None, 'dp')
- grad_down: bfloat16 [4, 4096, 2048], P('expert', 'dp')
The draws below stay inside these ranges and needn't reach their ends.
Inputs may be any that keep to these rules, and one draw needn't show every extreme that they name: `expert_ids`: within the 256 tokens of one group no expert is named more than 160 times; in some group's tokens one expert is named exactly 160 times.
All inputs are finite; a program needn't handle non-finite values.
Results may differ from the reference program's by a relative error of at most 0.012.
Values may be sent and summed in bfloat16 or wider, within the bound.
No kernel may reach another device: no remote copies, remote signals or barrier semaphores. Data moves between devices by JAX's collectives and lax.ppermute only.
A program may use at most 128 MiB of HBM per device.

```python
import math
import jax
import jax.numpy as jnp
import numpy as np
from jax import lax

D = 2048
FF = 4096
TOP = 1
TOK_DEV = 256
EXPERTS = 4
CAP = 160
TOKENS = 1024
N_DP = 8


def steps_of(rng, shape, cuts, smallest, top_value):
    factor_of, own = 1.0, jax.random.fold_in(rng, 6)
    for position, shards_of in cuts:
        heights = jnp.exp(jax.random.uniform(jax.random.fold_in(own, position), (shards_of,), jnp.float32, smallest / len(cuts), top_value / len(cuts)))
        factor_of = factor_of * jnp.repeat(heights, shape[position] // shards_of).reshape([-1 if axis == position else 1 for axis in range(len(shape))])
    return factor_of


def assign_block(stream_key, own, number, rows, number_of, top, bound, lean):
    order = jax.random.permutation(stream_key, number_of)
    packed, common = portions_of(number_of, rows * top, bound, lean, True), portions_of(number_of, rows * top, bound, lean, False)
    places = jnp.arange(number_of)

    def named(lengths, rotation):
        used = int((lengths > 0).sum())
        fixed = max(1, used // 4)
        shifted = fixed + (places - fixed + rotation * (used - fixed)) % max(1, number_of - fixed)
        return jnp.zeros((number_of,), jnp.int32).at[order[jnp.where(places < fixed, places, shifted)]].set(jnp.asarray(lengths, jnp.int32))

    lengths = jnp.where(number % 4 == 0, named(packed, number // 4), named(common, number - number // 4 - 1))
    mixed = jax.random.permutation(jax.random.fold_in(own, 3), number_of)
    source_of, sink = mixed[0:number_of // 2 * 2:2], mixed[1:number_of // 2 * 2:2]
    margin = jnp.minimum(lengths[source_of] - 1, bound - lengths[sink]) // 2
    margin = jnp.where((source_of == order[0]) | (sink == order[0]) | (lengths[sink] == 0), 0, jnp.maximum(margin, 0))
    shifted = jax.random.randint(jax.random.fold_in(own, 4), (number_of // 2,), 0, 1 << 20) % (margin + 1)
    lengths = lengths.at[source_of].add(-shifted).at[sink].add(shifted)
    labels = jnp.searchsorted(jnp.cumsum(lengths), jnp.arange(rows * top), side="right").astype(jnp.int32)
    listing = labels.reshape(top, rows).T
    listing = listing[jax.random.permutation(jax.random.fold_in(own, 1), rows)]
    rotation = jax.random.randint(jax.random.fold_in(own, 2), (rows, 1), 0, top)
    return jnp.take_along_axis(listing, (jnp.arange(top)[None, :] + rotation) % top, axis=1)


def portions_of(count, total, most, skew, full):
    weights = [(1 << 20) // math.isqrt(standing ** skew) + 1 for standing in range(1, count + 1)]
    largest = most if full else min(most, max(-(-total // count), total * weights[0] // sum(weights)))
    least = 1 if total - largest >= count - 1 else 0
    holding, rest = [largest] + [least] * (count - 1), total - largest - least * (count - 1)
    while rest > 0:
        candidates = [i for i in range(1, count) if holding[i] < largest] or [i for i in range(1, count) if holding[i] < most]
        whole, left = sum([weights[i] for i in candidates]), rest
        for i in candidates:
            more = min(most - holding[i], max(1, left * weights[i] // whole), rest)
            holding[i] = holding[i] + more
            rest = rest - more
    return np.array(holding)


def gaussian(stream_key, dims, width, reach, cuts=(), kind=jnp.bfloat16):
    values = jax.random.normal(stream_key, dims, jnp.float32) * width
    if len(cuts) > 0:
        values = steps_of(stream_key, dims, cuts, -0.22, 0.18) * values
    return jnp.clip(values, min=-reach, max=reach).astype(kind)


def setup_inputs(seed: int = 0) -> dict:
    seeds = jax.random.split(jax.random.key(seed), 8)
    tokens = gaussian(seeds[0], (TOKENS, D), 1.0, 6.0, ((0, 4),))
    grad_out = gaussian(seeds[1], (TOKENS, D), 1.0, 6.0, ((0, 4),))
    expert_ids_keys = jax.random.split(jax.random.fold_in(seeds[2], 1), TOKENS // TOK_DEV)
    expert_ids_turns = jax.random.permutation(jax.random.fold_in(seeds[2], 3), TOKENS // TOK_DEV)
    expert_ids = jax.vmap(lambda own, number: assign_block(jax.random.fold_in(seeds[2], 2), own, number, TOK_DEV, EXPERTS, TOP, CAP, 1))(expert_ids_keys, expert_ids_turns).reshape((TOKENS, TOP))
    gate_prob = jnp.clip(jnp.exp(math.log(1.0) - 1.609438 * jax.random.uniform(seeds[3], (TOKENS, TOP), jnp.float32) ** steps_of(seeds[3], (TOKENS, TOP), ((0, 4),), -0.2, 0.2)), 0.2, 1.0)
    w_gate = gaussian(seeds[4], (EXPERTS, D, FF), D ** -0.5, 0.125, ((0, 4), (2, 8)))
    w_up = gaussian(seeds[5], (EXPERTS, D, FF), D ** -0.5, 0.125, ((0, 4), (2, 8)))
    w_down = gaussian(seeds[6], (EXPERTS, FF, D), FF ** -0.5, 0.09375, ((0, 4), (1, 8)))
    return {"tokens": tokens, "grad_out": grad_out, "expert_ids": expert_ids, "gate_prob": gate_prob, "w_gate": w_gate, "w_up": w_up, "w_down": w_down}


def silu_parts(pre_gate):
    sigma = jax.nn.sigmoid(pre_gate)
    return pre_gate * sigma, sigma * (1.0 + pre_gate * (1.0 - sigma))


def reference(tokens, grad_out, expert_ids, gate_prob, w_gate, w_up, w_down):
    groups = TOKENS // TOK_DEV
    routed = expert_ids[:, 0].reshape(groups, TOK_DEV)
    one_hot = (routed[:, :, None] == jnp.arange(EXPERTS, dtype=jnp.int32)[None, None, :]).astype(jnp.int32)
    slot_index = jnp.sum((jnp.cumsum(one_hot, axis=1) - one_hot) * one_hot, axis=2).astype(jnp.int32)
    scaled = (gate_prob * grad_out.astype(jnp.float32)).astype(jnp.bfloat16)
    input_cube = tokens.astype(jnp.float32).reshape(groups, TOK_DEV, D)
    scaled_cube = scaled.astype(jnp.float32).reshape(groups, TOK_DEV, D)
    slot_range = jnp.arange(CAP, dtype=jnp.int32)
    blocks = N_DP
    block_width = FF // N_DP

    def per_expert(accum, expert):
        assign = ((routed[:, None, :] == expert) & (slot_index[:, None, :] == slot_range[None, :, None])).astype(jnp.float32)
        x_rows = jnp.einsum("dst,dtk->dsk", assign, input_cube).reshape(groups * CAP, D).astype(jnp.bfloat16)
        y_rows = jnp.einsum("dst,dtk->dsk", assign, scaled_cube).reshape(groups * CAP, D).astype(jnp.bfloat16)
        gate_w = w_gate[expert]
        up_w = w_up[expert]
        down_w = w_down[expert]
        pre_gate = jnp.dot(x_rows, gate_w, preferred_element_type=jnp.float32)
        pre_up = jnp.dot(x_rows, up_w, preferred_element_type=jnp.float32)
        activated, slope = silu_parts(pre_gate)
        hidden = (activated * pre_up).astype(jnp.bfloat16)
        hidden_grad = jnp.dot(y_rows, down_w.T, preferred_element_type=jnp.float32)
        down_grad = jnp.dot(hidden.T, y_rows, preferred_element_type=jnp.float32).astype(jnp.bfloat16)
        up_grad = (hidden_grad * activated).astype(jnp.bfloat16)
        gate_grad = (hidden_grad * pre_up * slope).astype(jnp.bfloat16)
        gate_wgrad = jnp.dot(x_rows.T, gate_grad, preferred_element_type=jnp.float32).astype(jnp.bfloat16)
        up_wgrad = jnp.dot(x_rows.T, up_grad, preferred_element_type=jnp.float32).astype(jnp.bfloat16)
        rows_all = groups * CAP
        gate_cube = gate_grad.astype(jnp.float32).reshape(rows_all, blocks, block_width)
        up_cube = up_grad.astype(jnp.float32).reshape(rows_all, blocks, block_width)
        gate_wcube = gate_w.astype(jnp.float32).reshape(D, blocks, block_width)
        up_wcube = up_w.astype(jnp.float32).reshape(D, blocks, block_width)
        partial_sums = jnp.einsum("rbf,dbf->brd", gate_cube, gate_wcube) + jnp.einsum("rbf,dbf->brd", up_cube, up_wcube)
        rounded = lax.optimization_barrier(partial_sums.astype(jnp.bfloat16))
        row_grad = jnp.sum(rounded.astype(jnp.float32), axis=0).astype(jnp.bfloat16)
        back = jnp.einsum("dst,dsk->dtk", assign, row_grad.astype(jnp.float32).reshape(groups, CAP, D))
        return accum + back, (gate_wgrad, up_wgrad, down_grad)

    start = jnp.zeros((groups, TOK_DEV, D), jnp.float32)
    total, stacked = lax.scan(per_expert, start, jnp.arange(EXPERTS, dtype=jnp.int32))
    grad_tokens = total.reshape(TOKENS, D).astype(jnp.bfloat16)
    return (grad_tokens, stacked[0], stacked[1], stacked[2])
```

```python
import functools
import jax
import jax.numpy as jnp
from jax import lax
from jax.experimental import pallas as pl
from jax.experimental.pallas import tpu as pltpu
from jax.sharding import PartitionSpec as P

BF16 = jnp.bfloat16
F32 = jnp.float32
LAST = (((1,), (1,)), ((), ()))
FIRST = (((0,), (0,)), ((), ()))
VMEM = pltpu.MemorySpace.VMEM


def silu_parts(pre_gate):
    sigma = jax.nn.sigmoid(pre_gate)
    return (pre_gate * sigma, sigma * (1.0 + pre_gate * (1.0 - sigma)))


def per_device_any(tokens, grad_out, expert_ids, gate_prob, w_gate, w_up, w_down):
    expert_count = lax.axis_size("expert")
    replica_count = lax.axis_size("dp")
    tok_count = tokens.shape[0]
    width_all = tokens.shape[1]
    capacity = max(2, (5 * tok_count + 2 * expert_count - 1) // (2 * expert_count))
    routed = expert_ids[:, 0]
    one_hot = (routed[:, None] == jnp.arange(expert_count, dtype=jnp.int32)[None, :]).astype(
        jnp.int32
    )
    slot_index = jnp.sum((jnp.cumsum(one_hot, axis=0) - one_hot) * one_hot, axis=1)
    target = routed * capacity + slot_index
    assign = (
        target[None, :] == jnp.arange(expert_count * capacity, dtype=jnp.int32)[:, None]
    ).astype(jnp.bfloat16)
    scaled = (gate_prob * grad_out.astype(jnp.float32)).astype(jnp.bfloat16)
    input_slots = jnp.dot(assign, tokens, preferred_element_type=jnp.float32).astype(jnp.bfloat16)
    scaled_slots = jnp.dot(assign, scaled, preferred_element_type=jnp.float32).astype(jnp.bfloat16)
    hidden_part = w_gate.shape[2]
    w_pair = jnp.concatenate([w_gate[0], w_up[0]], axis=1)
    down_rows = w_down[0]
    contract_last = (((1,), (1,)), ((), ()))
    contract_first = (((0,), (0,)), ((), ()))
    share = width_all // replica_count
    offset = lax.axis_index("dp") * share
    input_cols = lax.dynamic_slice_in_dim(input_slots, offset, share, 1)
    scaled_cols = lax.dynamic_slice_in_dim(scaled_slots, offset, share, 1)
    got_input, got_scaled = (
        lax.all_to_all(input_cols, "expert", split_axis=0, concat_axis=0, tiled=True),
        lax.all_to_all(scaled_cols, "expert", split_axis=0, concat_axis=0, tiled=True),
    )
    all_inputs, all_scaled = (
        lax.all_gather(got_input, "dp", axis=1, tiled=True),
        lax.all_gather(got_scaled, "dp", axis=1, tiled=True),
    )
    pre_act = jnp.dot(all_inputs, w_pair, preferred_element_type=jnp.float32)
    pre_gate = pre_act[:, :hidden_part]
    pre_up = pre_act[:, hidden_part:]
    activated, slope = silu_parts(pre_gate)
    hidden = (activated * pre_up).astype(jnp.bfloat16)
    hidden_grad = lax.dot_general(
        all_scaled, down_rows, contract_last, preferred_element_type=jnp.float32
    )
    down_grad = lax.dot_general(
        hidden, all_scaled, contract_first, preferred_element_type=jnp.float32
    )
    up_grad = (hidden_grad * activated).astype(jnp.bfloat16)
    gate_grad = (hidden_grad * pre_up * slope).astype(jnp.bfloat16)
    pair_grad = jnp.concatenate([gate_grad, up_grad], axis=1)
    weight_grad = lax.dot_general(
        all_inputs, pair_grad, contract_first, preferred_element_type=jnp.float32
    )
    terms = lax.dot_general(pair_grad, w_pair, contract_last, preferred_element_type=jnp.float32)
    weight_grad, down_grad, terms = (weight_grad, down_grad, terms)
    summed = lax.psum_scatter(terms.astype(jnp.bfloat16), "dp", scatter_dimension=1, tiled=True)
    returned_rows = lax.all_to_all(summed, "expert", split_axis=0, concat_axis=0, tiled=True)
    token_cols = lax.dot_general(
        assign, returned_rows, contract_first, preferred_element_type=jnp.float32
    ).astype(jnp.bfloat16)
    grad_tokens = lax.all_gather(token_cols, "dp", axis=1, tiled=True)
    gate_wgrad = weight_grad[:, :hidden_part].astype(jnp.bfloat16)
    up_wgrad = weight_grad[:, hidden_part:].astype(jnp.bfloat16)
    return (grad_tokens, gate_wgrad[None], up_wgrad[None], down_grad.astype(jnp.bfloat16)[None])


def call(body, outs, operands, flops, limit, scratch=()):
    nbytes = sum(a.size * a.dtype.itemsize for a in operands)
    nbytes += sum(o.size * o.dtype.itemsize for o in outs)
    return pl.pallas_call(
        body,
        out_shape=outs,
        in_specs=[pl.BlockSpec(memory_space=VMEM)] * len(operands),
        out_specs=[pl.BlockSpec(memory_space=VMEM)] * len(outs),
        scratch_shapes=list(scratch),
        compiler_params=pltpu.CompilerParams(vmem_limit_bytes=limit << 20),
        cost_estimate=pl.CostEstimate(flops=flops, bytes_accessed=nbytes, transcendentals=0),
    )(*operands)


def shape(*dims, dtype=BF16):
    return jax.ShapeDtypeStruct(dims, dtype)


def cols(block, width):
    return pl.ds(pl.multiple_of(block * width, width), width)


def dispatch_kernel(capacity, share, tok, grad, ids, prob, send1, send2, send3, own, back):
    here = lax.axis_index("expert")
    block = lax.axis_index("dp")
    count = tok.shape[0]
    relative = jnp.bitwise_xor(ids[...], here)
    lane = lax.broadcasted_iota(jnp.int32, (count, 128), 1)
    hit = (relative == lane).astype(F32)
    row = lax.broadcasted_iota(jnp.int32, (count, count), 0)
    col = lax.broadcasted_iota(jnp.int32, (count, count), 1)
    earlier = (col < row).astype(BF16)
    before = jnp.dot(earlier, hit.astype(BF16), preferred_element_type=F32)
    slot = jnp.sum(before * hit, axis=1, keepdims=True)
    target = relative.astype(F32) * capacity + slot
    places = own.shape[0] * 4
    spots = lax.broadcasted_iota(jnp.int32, (count, places), 1)
    target_int = target.astype(jnp.int32)
    back[...] = (target_int == spots).astype(F32).astype(BF16)
    across = jnp.transpose(jnp.broadcast_to(target, (count, 128)))[0:1, :].astype(jnp.int32)
    spots_t = lax.broadcasted_iota(jnp.int32, (places, count), 0)
    assign = (across == spots_t).astype(F32).astype(BF16)
    own[...] = assign[:capacity]
    x_part = tok[:, cols(block, share)]
    y_part = (prob[...] * grad[:, cols(block, share)].astype(F32)).astype(BF16)
    for k, ref in ((1, send1), (2, send2), (3, send3)):
        pick = assign[k * capacity : (k + 1) * capacity]
        ref[:capacity] = jnp.dot(pick, x_part, preferred_element_type=F32).astype(BF16)
        ref[capacity:] = jnp.dot(pick, y_part, preferred_element_type=F32).astype(BF16)


def expert_math(share, x_all, y_all, w_gate, w_up, w_down, hidden, gate_grad, up_grad, even, odd):
    block = lax.axis_index("dp")
    rows = x_all.shape[0]
    pre_gate = jnp.dot(x_all[...], w_gate[...], preferred_element_type=F32)
    pre_up = jnp.dot(x_all[...], w_up[...], preferred_element_type=F32)
    hidden_grad = lax.dot_general(y_all[...], w_down[...], LAST, preferred_element_type=F32)
    activated, slope = silu_parts(pre_gate)
    hidden[...] = (activated * pre_up).astype(BF16)
    gate_grad[...] = (hidden_grad * pre_up * slope).astype(BF16)
    up_grad[...] = (hidden_grad * activated).astype(BF16)
    for k in range(8):
        piece = cols(jnp.bitwise_xor(block, k), share)
        term = lax.dot_general(gate_grad[...], w_gate[piece, :], LAST, preferred_element_type=F32)
        term += lax.dot_general(up_grad[...], w_up[piece, :], LAST, preferred_element_type=F32)
        (odd if k % 2 else even)[k // 2] = term.astype(BF16)


def own_kernel(share, tok, grad, prob, own, w_gate, w_up, w_down, x_all, y_all, *rest):
    scaled = (prob[...] * grad[...].astype(F32)).astype(BF16)
    x_all[...] = jnp.dot(own[...], tok[...], preferred_element_type=F32).astype(BF16)
    y_all[...] = jnp.dot(own[...], scaled, preferred_element_type=F32).astype(BF16)
    expert_math(share, x_all, y_all, w_gate, w_up, w_down, *rest)


def chunk_kernel(share, *refs):
    blocks, halves, rest = refs[:6], refs[6:10], refs[10:]
    w_gate, w_up, w_down, x_all, y_all = rest[:5]
    block = lax.axis_index("dp")
    rows = x_all.shape[0]
    for k, ref in enumerate(blocks):
        piece = cols(jnp.bitwise_xor(block, k), share)
        x_all[:, piece] = ref[:rows]
        y_all[:, piece] = ref[rows:]
    for k in (6, 7):
        piece = cols(jnp.bitwise_xor(block, k), share)
        x_all[:, piece] = halves[2 * (k - 6)][...]
        y_all[:, piece] = halves[2 * (k - 6) + 1][...]
    expert_math(share, x_all, y_all, w_gate, w_up, w_down, *rest[5:])


def pair_wgrad_kernel(x0, x1, x2, g0, g1, g2, u0, u1, u2, gate_out, up_out):
    gate = 0.0
    up = 0.0
    for x, g, u in ((x0, g0, u0), (x1, g1, u1), (x2, g2, u2)):
        gate += lax.dot_general(x[...], g[...], FIRST, preferred_element_type=F32)
        up += lax.dot_general(x[...], u[...], FIRST, preferred_element_type=F32)
    gate_out[...] = gate.astype(BF16)
    up_out[...] = up.astype(BF16)


def wgrad_kernel(a0, a1, a2, b0, b1, b2, out):
    total = lax.dot_general(a0[...], b0[...], FIRST, preferred_element_type=F32)
    total += lax.dot_general(a1[...], b1[...], FIRST, preferred_element_type=F32)
    total += lax.dot_general(a2[...], b2[...], FIRST, preferred_element_type=F32)
    out[...] = total.astype(BF16)


def combine_kernel(back, r0, r1, r2, r3, out, rows):
    capacity = r0.shape[0]
    for k, ref in enumerate((r0, r1, r2, r3)):
        rows[k * capacity : (k + 1) * capacity] = ref[...]
    out[...] = jnp.dot(back[...], rows[...], preferred_element_type=F32).astype(BF16)


def place_kernel(share, *refs):
    out = refs[-1]
    block = lax.axis_index("dp")
    half = out.shape[0] // 2
    for k, ref in enumerate(refs[:6]):
        out[:, cols(jnp.bitwise_xor(block, k), share)] = ref[...]
    for k in (6, 7):
        piece = cols(jnp.bitwise_xor(block, k), share)
        out[:half, piece] = refs[2 * k - 6][...]
        out[half:, piece] = refs[2 * k - 5][...]


def swap(array, axis, distance):
    size = lax.axis_size(axis)
    return lax.ppermute(array, axis, [(i, i ^ distance) for i in range(size)])


def gather_blocks(block):
    half = block.shape[0] // 2
    by_two = swap(block, "dp", 2)
    by_four = swap(block, "dp", 4)
    first = swap(by_two[:half], "dp", 4)
    second = swap(by_four[half:], "dp", 2)
    return (
        block,
        swap(block, "dp", 1),
        by_two,
        swap(by_two, "dp", 1),
        by_four,
        swap(by_four, "dp", 1),
        first,
        second,
        swap(first, "dp", 1),
        swap(second, "dp", 1),
    )


def scatter_blocks(even, odd):
    other = swap(odd, "dp", 1)
    pair = [(even[j].astype(F32) + other[j].astype(F32)).astype(BF16) for j in range(4)]
    total = pair[0].astype(F32)
    for j in range(1, 4):
        total += swap(pair[j], "dp", 2 * j).astype(F32)
    return total.astype(BF16)


def expert_outs(rows, width, hidden, share):
    return [
        shape(rows, width),
        shape(rows, width),
        shape(rows, hidden),
        shape(rows, hidden),
        shape(rows, hidden),
        shape(4, rows, share),
        shape(4, rows, share),
    ]


def per_device_blocks(tokens, grad_out, expert_ids, gate_prob, w_gate, w_up, w_down):
    count, width = tokens.shape
    experts = lax.axis_size("expert")
    share = width // lax.axis_size("dp")
    capacity = max(2, (5 * count + 2 * experts - 1) // (2 * experts))
    hidden_part = w_gate.shape[2]
    weights = (w_gate[0], w_up[0], w_down[0])

    send1, send2, send3, own, back = call(
        functools.partial(dispatch_kernel, capacity, share),
        [shape(2 * capacity, share)] * 3
        + [shape(capacity, count), shape(count, experts * capacity)],
        (tokens, grad_out, expert_ids, gate_prob),
        4 * 3 * capacity * count * share,
        8,
    )
    got1 = swap(send1, "expert", 1)
    got3 = swap(send3, "expert", 3)
    got2 = swap(send2, "expert", 2)

    def math_flops(rows):
        return 10 * rows * width * hidden_part

    own_out = call(
        functools.partial(own_kernel, share),
        expert_outs(capacity, width, hidden_part, share),
        (tokens, grad_out, gate_prob, own) + weights,
        math_flops(capacity),
        16,
    )
    ret0 = scatter_blocks(own_out[5], own_out[6])

    block_a = jnp.concatenate(
        [got1[:capacity], got3[:capacity], got1[capacity:], got3[capacity:]], axis=0
    )
    blocks_a = gather_blocks(block_a)
    out_a = call(
        functools.partial(chunk_kernel, share),
        expert_outs(2 * capacity, width, hidden_part, share),
        blocks_a + weights,
        math_flops(2 * capacity),
        16,
    )
    summed_a = scatter_blocks(out_a[5], out_a[6])
    ret1 = swap(summed_a[:capacity], "expert", 1)
    ret3 = swap(summed_a[capacity:], "expert", 3)

    blocks_b = gather_blocks(got2)
    out_b = call(
        functools.partial(chunk_kernel, share),
        expert_outs(capacity, width, hidden_part, share),
        blocks_b + weights,
        math_flops(capacity),
        16,
    )
    ret2 = swap(scatter_blocks(out_b[5], out_b[6]), "expert", 2)

    (token_cols,) = call(
        combine_kernel,
        [shape(count, share)],
        (back, ret0, ret1, ret2, ret3),
        2 * count * experts * capacity * share,
        8,
        [pltpu.VMEM((experts * capacity, share), BF16)],
    )
    (grad_tokens,) = call(
        functools.partial(place_kernel, share),
        [shape(count, width)],
        gather_blocks(token_cols),
        count * width,
        8,
    )
    parts = (own_out, out_a, out_b)
    rows_all = experts * capacity
    gate_wgrad, up_wgrad = call(
        pair_wgrad_kernel,
        [shape(width, hidden_part)] * 2,
        [o[0] for o in parts] + [o[3] for o in parts] + [o[4] for o in parts],
        4 * rows_all * width * hidden_part,
        24,
    )
    (down_wgrad,) = call(
        wgrad_kernel,
        [shape(hidden_part, width)],
        [o[2] for o in parts] + [o[1] for o in parts],
        2 * rows_all * width * hidden_part,
        16,
    )
    return (grad_tokens, gate_wgrad[None], up_wgrad[None], down_wgrad[None])


def solution(mesh):
    placed = (
        P("expert", None),
        P("expert", None),
        P("expert", None),
        P("expert", None),
        P("expert", None, "dp"),
        P("expert", None, "dp"),
        P("expert", "dp", None),
    )
    fits = mesh.shape["dp"] == 8 and mesh.shape["expert"] == 4
    return jax.shard_map(
        per_device_blocks if fits else per_device_any,
        mesh=mesh,
        in_specs=placed,
        out_specs=(
            P("expert", None),
            P("expert", None, "dp"),
            P("expert", None, "dp"),
            P("expert", "dp", None),
        ),
        check_vma=False,
    )
```

```python
import functools
import jax
import jax.numpy as jnp
from jax import lax
from jax.experimental import pallas as pl
from jax.experimental.pallas import tpu as pltpu
from jax.sharding import PartitionSpec as P

BF16 = jnp.bfloat16
F32 = jnp.float32
LAST = (((1,), (1,)), ((), ()))
FIRST = (((0,), (0,)), ((), ()))
VMEM = pltpu.MemorySpace.VMEM


def silu_parts(pre_gate):
    sigma = jax.nn.sigmoid(pre_gate)
    return (pre_gate * sigma, sigma * (1.0 + pre_gate * (1.0 - sigma)))


def per_device_any(tokens, grad_out, expert_ids, gate_prob, w_gate, w_up, w_down):
    expert_count = lax.axis_size("expert")
    replica_count = lax.axis_size("dp")
    tok_count = tokens.shape[0]
    width_all = tokens.shape[1]
    capacity = max(2, (5 * tok_count + 2 * expert_count - 1) // (2 * expert_count))
    routed = expert_ids[:, 0]
    one_hot = (routed[:, None] == jnp.arange(expert_count, dtype=jnp.int32)[None, :]).astype(
        jnp.int32
    )
    slot_index = jnp.sum((jnp.cumsum(one_hot, axis=0) - one_hot) * one_hot, axis=1)
    target = routed * capacity + slot_index
    assign = (
        target[None, :] == jnp.arange(expert_count * capacity, dtype=jnp.int32)[:, None]
    ).astype(jnp.bfloat16)
    scaled = (gate_prob * grad_out.astype(jnp.float32)).astype(jnp.bfloat16)
    input_slots = jnp.dot(assign, tokens, preferred_element_type=jnp.float32).astype(jnp.bfloat16)
    scaled_slots = jnp.dot(assign, scaled, preferred_element_type=jnp.float32).astype(jnp.bfloat16)
    hidden_part = w_gate.shape[2]
    w_pair = jnp.concatenate([w_gate[0], w_up[0]], axis=1)
    down_rows = w_down[0]
    contract_last = (((1,), (1,)), ((), ()))
    contract_first = (((0,), (0,)), ((), ()))
    share = width_all // replica_count
    offset = lax.axis_index("dp") * share
    input_cols = lax.dynamic_slice_in_dim(input_slots, offset, share, 1)
    scaled_cols = lax.dynamic_slice_in_dim(scaled_slots, offset, share, 1)
    got_input, got_scaled = (
        lax.all_to_all(input_cols, "expert", split_axis=0, concat_axis=0, tiled=True),
        lax.all_to_all(scaled_cols, "expert", split_axis=0, concat_axis=0, tiled=True),
    )
    all_inputs, all_scaled = (
        lax.all_gather(got_input, "dp", axis=1, tiled=True),
        lax.all_gather(got_scaled, "dp", axis=1, tiled=True),
    )
    pre_act = jnp.dot(all_inputs, w_pair, preferred_element_type=jnp.float32)
    pre_gate = pre_act[:, :hidden_part]
    pre_up = pre_act[:, hidden_part:]
    activated, slope = silu_parts(pre_gate)
    hidden = (activated * pre_up).astype(jnp.bfloat16)
    hidden_grad = lax.dot_general(
        all_scaled, down_rows, contract_last, preferred_element_type=jnp.float32
    )
    down_grad = lax.dot_general(
        hidden, all_scaled, contract_first, preferred_element_type=jnp.float32
    )
    up_grad = (hidden_grad * activated).astype(jnp.bfloat16)
    gate_grad = (hidden_grad * pre_up * slope).astype(jnp.bfloat16)
    pair_grad = jnp.concatenate([gate_grad, up_grad], axis=1)
    weight_grad = lax.dot_general(
        all_inputs, pair_grad, contract_first, preferred_element_type=jnp.float32
    )
    terms = lax.dot_general(pair_grad, w_pair, contract_last, preferred_element_type=jnp.float32)
    weight_grad, down_grad, terms = (weight_grad, down_grad, terms)
    summed = lax.psum_scatter(terms.astype(jnp.bfloat16), "dp", scatter_dimension=1, tiled=True)
    returned_rows = lax.all_to_all(summed, "expert", split_axis=0, concat_axis=0, tiled=True)
    token_cols = lax.dot_general(
        assign, returned_rows, contract_first, preferred_element_type=jnp.float32
    ).astype(jnp.bfloat16)
    grad_tokens = lax.all_gather(token_cols, "dp", axis=1, tiled=True)
    gate_wgrad = weight_grad[:, :hidden_part].astype(jnp.bfloat16)
    up_wgrad = weight_grad[:, hidden_part:].astype(jnp.bfloat16)
    return (grad_tokens, gate_wgrad[None], up_wgrad[None], down_grad.astype(jnp.bfloat16)[None])


SMALL = 1000
HBM = pltpu.MemorySpace.HBM


def call(body, outs, operands, flops, limit, scratch=(), far=0, aliases=None):
    nbytes = sum(a.size * a.dtype.itemsize for a in operands)
    nbytes += sum(o.size * o.dtype.itemsize for o in outs)
    return pl.pallas_call(
        body,
        out_shape=outs,
        in_specs=[pl.BlockSpec(memory_space=HBM)] * far
        + [pl.BlockSpec(memory_space=VMEM)] * (len(operands) - far),
        out_specs=[pl.BlockSpec(memory_space=VMEM)] * len(outs),
        scratch_shapes=list(scratch),
        input_output_aliases=aliases or {},
        compiler_params=pltpu.CompilerParams(vmem_limit_bytes=limit << 20),
        cost_estimate=pl.CostEstimate(flops=flops, bytes_accessed=nbytes, transcendentals=0),
    )(*[pltpu.with_memory_space_constraint(a, HBM) for a in operands[:far]], *operands[far:])


def shape(*dims, dtype=BF16):
    return jax.ShapeDtypeStruct(dims, dtype)


def cols(block, width):
    return pl.ds(pl.multiple_of(block * width, width), width)


def column(row):
    return jnp.transpose(jnp.broadcast_to(row, (128, row.shape[1])))[:, 0:1]


def start_copies(sems, *pairs):
    copies = [pltpu.make_async_copy(src, dst, sems.at[j]) for j, (src, dst) in enumerate(pairs)]
    for copy in copies:
        copy.start()
    return copies


def dispatch_kernel(
    capacity, share, ids_far, prob_far, tok, grad, send1, send2, send3, assign,
    ids, prob, tok_part, grad_part, sems,
):
    here = lax.axis_index("expert")
    piece = cols(lax.axis_index("dp"), share)
    ids_copy, prob_copy, tok_copy, grad_copy = start_copies(
        sems,
        (ids_far, ids),
        (prob_far, prob),
        (tok.at[:, piece], tok_part),
        (grad.at[:, piece], grad_part),
    )
    ids_copy.wait()
    count = tok.shape[0]
    places = assign.shape[0]
    relative = jnp.bitwise_xor(ids[...], here)
    expert = lax.broadcasted_iota(jnp.int32, (8, count), 0)
    hit = (relative == expert).astype(F32)
    row = lax.broadcasted_iota(jnp.int32, (count, count), 0)
    col = lax.broadcasted_iota(jnp.int32, (count, count), 1)
    earlier = (row < col).astype(F32).astype(BF16)
    before = jnp.dot(hit.astype(BF16), earlier, preferred_element_type=F32)
    slot = jnp.sum(before * hit, axis=0, keepdims=True).astype(jnp.int32)
    target = relative * capacity + slot
    spots = lax.broadcasted_iota(jnp.int32, (places, count), 0)
    assign[...] = (target == spots).astype(F32).astype(BF16)
    prob_copy.wait()
    weight = column(prob[...])
    tok_copy.wait()
    for k, ref in ((1, send1), (3, send3), (2, send2)):
        pick = assign[k * capacity : (k + 1) * capacity]
        ref[:capacity] = jnp.dot(pick, tok_part[...], preferred_element_type=F32).astype(BF16)
    grad_copy.wait()
    y_part = (weight * grad_part[...].astype(F32)).astype(BF16)
    for k, ref in ((1, send1), (3, send3), (2, send2)):
        pick = assign[k * capacity : (k + 1) * capacity]
        ref[capacity:] = jnp.dot(pick, y_part, preferred_element_type=F32).astype(BF16)


def expert_math(
    share, start, x_all, y_all, w_gate, w_up, w_down, hidden, gate_grad, up_grad, even, odd,
    ready=(lambda: None,) * 3,
):
    block = lax.axis_index("dp")
    rows = x_all.shape[0]
    ready[0]()
    pre_gate = jnp.dot(x_all[...], w_gate[...], preferred_element_type=F32)
    ready[1]()
    pre_up = jnp.dot(x_all[...], w_up[...], preferred_element_type=F32)
    ready[2]()
    hidden_grad = lax.dot_general(y_all[...], w_down[...], LAST, preferred_element_type=F32)
    activated, slope = silu_parts(pre_gate)
    hidden[...] = (activated * pre_up).astype(BF16)
    gate_grad[...] = (hidden_grad * pre_up * slope).astype(BF16)
    up_grad[...] = (hidden_grad * activated).astype(BF16)
    for k in range(8):
        piece = cols(jnp.bitwise_xor(block, k), share)
        term = lax.dot_general(gate_grad[...], w_gate[piece, :], LAST, preferred_element_type=F32)
        term += lax.dot_general(up_grad[...], w_up[piece, :], LAST, preferred_element_type=F32)
        (odd if k % 2 else even)[k // 2, start : start + rows] = term.astype(BF16)


def own_kernel(
    share, start, prob_far, tok_far, grad_far, gate_far, up_far, down_far, assign,
    x_all, y_all, hidden, gate_grad, up_grad, even, odd, w_gate, w_up, w_down,
    prob, tok, grad, sems,
):
    prob_copy, tok_copy, grad_copy, *weight_copies = start_copies(
        sems,
        (prob_far, prob),
        (tok_far, tok),
        (grad_far, grad),
        (gate_far, w_gate),
        (up_far, w_up),
        (down_far, w_down),
    )
    own = assign[: x_all.shape[0]]
    tok_copy.wait()
    x_all[...] = jnp.dot(own, tok[...], preferred_element_type=F32).astype(BF16)
    prob_copy.wait()
    grad_copy.wait()
    scaled = (column(prob[...]) * grad[...].astype(F32)).astype(BF16)
    y_all[...] = jnp.dot(own, scaled, preferred_element_type=F32).astype(BF16)
    expert_math(
        share, start, x_all, y_all, w_gate, w_up, w_down, hidden, gate_grad, up_grad, even, odd,
        [copy.wait for copy in weight_copies],
    )


def chunk_kernel(share, extra, *refs):
    block_ref, by_two, by_four, first, second, across = refs[:6]
    rest = refs[6 + extra :]
    w_gate, w_up, w_down, x_all, y_all = rest[:5]
    block = lax.axis_index("dp")
    half = block_ref.shape[0] // 2
    near = [halves_of(ref) for ref in parts_of(across, 4)]
    mine = [halves_of(block_ref), halves_of(by_two), halves_of(by_four), (first, second)]
    for k in range(8):
        x_part, y_part = (near if k % 2 else mine)[k // 2]
        piece = cols(jnp.bitwise_xor(block, k), share)
        x_all[:, piece] = x_part[...]
        y_all[:, piece] = y_part[...]
    expert_math(share, 0, x_all, y_all, w_gate, w_up, w_down, *rest[5:])


def wgrad_kernel(a0, a1, a2, b0, b1, b2, out):
    total = lax.dot_general(a0[...], b0[...], FIRST, preferred_element_type=F32)
    total += lax.dot_general(a1[...], b1[...], FIRST, preferred_element_type=F32)
    total += lax.dot_general(a2[...], b2[...], FIRST, preferred_element_type=F32)
    out[...] = total.astype(BF16)


def combine_kernel(assign, r0, r1, r2, r3, out, rows):
    capacity = r0.shape[0]
    for k, ref in enumerate((r0, r1, r2, r3)):
        rows[k * capacity : (k + 1) * capacity] = ref[...]
    out[...] = lax.dot_general(assign[...], rows[...], FIRST, preferred_element_type=F32).astype(BF16)


def place_kernel(share, *refs):
    out = refs[-1]
    block = lax.axis_index("dp")
    near = parts_of(refs[4], 4)
    for k in range(8):
        piece = cols(jnp.bitwise_xor(block, k), share)
        out[:, piece] = (near if k % 2 else refs)[k // 2][...]


def fence(*arrays):
    return lax.optimization_barrier(arrays)


def swap(array, axis, distance):
    size = lax.axis_size(axis)
    return lax.ppermute(array, axis, [(i, i ^ distance) for i in range(size)])


def halves_of(ref):
    half = ref.shape[0] // 2
    return (ref.at[pl.ds(0, half)], ref.at[pl.ds(half, half)])


def parts_of(ref, count):
    rows = ref.shape[0] // count
    return [ref.at[pl.ds(j * rows, rows)] for j in range(count)]


def core_pairs(even, other):
    return [(even[j].astype(F32) + other[j].astype(F32)).astype(BF16) for j in range(4)]


def total_of(parts):
    return sum(part.astype(F32) for part in parts).astype(BF16)


def expert_outs(rows, width, hidden, share, all_rows=None):
    return [
        shape(rows, width),
        shape(rows, width),
        shape(rows, hidden),
        shape(rows, hidden),
        shape(rows, hidden),
        shape(4, all_rows or rows, share),
        shape(4, all_rows or rows, share),
    ]


def per_device_blocks(tokens, grad_out, expert_ids, gate_prob, w_gate, w_up, w_down):
    count, width = tokens.shape
    experts = lax.axis_size("expert")
    share = width // lax.axis_size("dp")
    capacity = max(2, (5 * count + 2 * experts - 1) // (2 * experts))
    hidden_part = w_gate.shape[2]
    weights = (w_gate[0], w_up[0], w_down[0])

    ids = expert_ids.T
    prob = gate_prob.T
    send1, send2, send3, assign = call(
        functools.partial(dispatch_kernel, capacity, share),
        [shape(2 * capacity, share)] * 3 + [shape(experts * capacity, count)],
        (ids, prob, tokens, grad_out),
        SMALL,
        8,
        [pltpu.VMEM((1, count), jnp.int32), pltpu.VMEM((1, count), F32)]
        + [pltpu.VMEM((count, share), BF16)] * 2
        + [pltpu.SemaphoreType.DMA((4,))],
        far=4,
    )
    got1 = swap(send1, "expert", 1)
    got3 = swap(send3, "expert", 3)
    own_out = call(
        functools.partial(own_kernel, share, 2 * capacity),
        expert_outs(capacity, width, hidden_part, share, 3 * capacity)
        + [shape(*w.shape) for w in weights],
        (prob, tokens, grad_out) + weights + (assign,),
        SMALL,
        20,
        [pltpu.VMEM((1, count), F32)]
        + [pltpu.VMEM((count, width), BF16)] * 2
        + [pltpu.SemaphoreType.DMA((6,))],
        far=6,
    )
    send2, *own_out = fence(send2, *own_out)
    block_b = swap(send2, "expert", 2)
    got1, got3, *own_out = fence(got1, got3, *own_out)
    weights = tuple(own_out[7:])

    block_a = jnp.concatenate(
        [got1[:capacity], got3[:capacity], got1[capacity:], got3[capacity:]], axis=0
    )
    half_a, half_b = 2 * capacity, capacity
    two_a = swap(block_a, "dp", 2)
    four_a = swap(block_a, "dp", 4)
    block_a, two_a, four_a, block_b = fence(block_a, two_a, four_a, block_b)

    first_a = swap(two_a[:half_a], "dp", 4)
    second_a = swap(four_a[half_a:], "dp", 2)
    two_b = swap(block_b, "dp", 2)
    four_b = swap(block_b, "dp", 4)
    first_a, second_a, two_b, four_b = fence(first_a, second_a, two_b, four_b)

    across_a = swap(jnp.concatenate([block_a, two_a, four_a, first_a, second_a]), "dp", 1)
    first_b = swap(two_b[:half_b], "dp", 4)
    second_b = swap(four_b[half_b:], "dp", 2)
    out_a = call(
        functools.partial(chunk_kernel, share, 2),
        expert_outs(2 * capacity, width, hidden_part, share, 3 * capacity),
        (block_a, two_a, four_a, first_a, second_a, across_a, own_out[5], own_out[6]) + weights,
        SMALL,
        16,
        aliases={6: 5, 7: 6},
    )
    first_b, second_b, *out_a = fence(first_b, second_b, *out_a)

    other_a = swap(out_a[6], "dp", 1)
    across_b = swap(jnp.concatenate([block_b, two_b, four_b, first_b, second_b]), "dp", 1)
    other_a, across_b = fence(other_a, across_b)

    pairs_a = core_pairs(out_a[5], other_a)
    sums_a = [swap(pairs_a[j], "dp", 2 * j) for j in range(1, 4)]
    out_b = call(
        functools.partial(chunk_kernel, share, 0),
        expert_outs(capacity, width, hidden_part, share),
        (block_b, two_b, four_b, first_b, second_b, across_b) + weights,
        SMALL,
        16,
    )
    out_b = fence(*out_b)
    sums_a[0], *rest = fence(sums_a[0], swap(out_b[6], "dp", 1), *out_b)
    other_b, out_b = rest[0], rest[1:]

    parts = (own_out, out_a, out_b)
    rows_all = experts * capacity

    def wgrad(left, right, rows, width_out):
        (out,) = call(
            wgrad_kernel,
            [shape(rows, width_out)],
            [o[left] for o in parts] + [o[right] for o in parts],
            2 * rows_all * rows * width_out,
            16,
        )
        return out

    pairs_b = core_pairs(out_b[5], other_b)
    sums_b = [swap(pairs_b[j], "dp", 2 * j) for j in range(1, 4)]
    gate_wgrad = wgrad(0, 3, width, hidden_part)
    *rest, gate_wgrad = fence(*sums_a, *sums_b, gate_wgrad)
    sums_a, sums_b = rest[:3], rest[3:]

    summed_a = total_of([pairs_a[0]] + sums_a)
    ret0 = summed_a[2 * capacity :]
    ret1 = swap(summed_a[:capacity], "expert", 1)
    ret3 = swap(summed_a[capacity : 2 * capacity], "expert", 3)
    ret2 = swap(total_of([pairs_b[0]] + sums_b), "expert", 2)
    up_wgrad = wgrad(0, 4, width, hidden_part)
    ret1, ret2, ret3, up_wgrad = fence(ret1, ret2, ret3, up_wgrad)
    (token_cols,) = call(
        combine_kernel,
        [shape(count, share)],
        (assign, ret0, ret1, ret2, ret3),
        SMALL,
        8,
        [pltpu.VMEM((experts * capacity, share), BF16)],
    )
    down_wgrad = wgrad(2, 1, hidden_part, width)
    six = swap(token_cols, "dp", 6)
    two = swap(token_cols, "dp", 2)
    four = swap(token_cols, "dp", 4)
    two, four, six, down_wgrad = fence(two, four, six, down_wgrad)
    across = swap(jnp.concatenate([token_cols, two, four, six]), "dp", 1)
    (grad_tokens,) = call(
        functools.partial(place_kernel, share),
        [shape(count, width)],
        (token_cols, two, four, six, across),
        SMALL,
        8,
    )
    return (grad_tokens, gate_wgrad[None], up_wgrad[None], down_wgrad[None])


def solution(mesh):
    placed = (
        P("expert", None),
        P("expert", None),
        P("expert", None),
        P("expert", None),
        P("expert", None, "dp"),
        P("expert", None, "dp"),
        P("expert", "dp", None),
    )
    fits = mesh.shape["dp"] == 8 and mesh.shape["expert"] == 4
    return jax.shard_map(
        per_device_blocks if fits else per_device_any,
        mesh=mesh,
        in_specs=placed,
        out_specs=(
            P("expert", None),
            P("expert", None, "dp"),
            P("expert", None, "dp"),
            P("expert", "dp", None),
        ),
        check_vma=False,
    )
```

```python
import functools
import jax
import jax.numpy as jnp
from jax import lax
from jax.experimental import pallas as pl
from jax.experimental.pallas import tpu as pltpu
from jax.sharding import PartitionSpec as P

BF16 = jnp.bfloat16
F32 = jnp.float32
LAST = (((1,), (1,)), ((), ()))
FIRST = (((0,), (0,)), ((), ()))
VMEM = pltpu.MemorySpace.VMEM


def silu_parts(pre_gate):
    sigma = jax.nn.sigmoid(pre_gate)
    return (pre_gate * sigma, sigma * (1.0 + pre_gate * (1.0 - sigma)))


def per_device_any(tokens, grad_out, expert_ids, gate_prob, w_gate, w_up, w_down):
    expert_count = lax.axis_size("expert")
    replica_count = lax.axis_size("dp")
    tok_count = tokens.shape[0]
    width_all = tokens.shape[1]
    capacity = max(2, (5 * tok_count + 2 * expert_count - 1) // (2 * expert_count))
    routed = expert_ids[:, 0]
    one_hot = (routed[:, None] == jnp.arange(expert_count, dtype=jnp.int32)[None, :]).astype(
        jnp.int32
    )
    slot_index = jnp.sum((jnp.cumsum(one_hot, axis=0) - one_hot) * one_hot, axis=1)
    target = routed * capacity + slot_index
    assign = (
        target[None, :] == jnp.arange(expert_count * capacity, dtype=jnp.int32)[:, None]
    ).astype(jnp.bfloat16)
    scaled = (gate_prob * grad_out.astype(jnp.float32)).astype(jnp.bfloat16)
    input_slots = jnp.dot(assign, tokens, preferred_element_type=jnp.float32).astype(jnp.bfloat16)
    scaled_slots = jnp.dot(assign, scaled, preferred_element_type=jnp.float32).astype(jnp.bfloat16)
    hidden_part = w_gate.shape[2]
    w_pair = jnp.concatenate([w_gate[0], w_up[0]], axis=1)
    down_rows = w_down[0]
    contract_last = (((1,), (1,)), ((), ()))
    contract_first = (((0,), (0,)), ((), ()))
    share = width_all // replica_count
    offset = lax.axis_index("dp") * share
    input_cols = lax.dynamic_slice_in_dim(input_slots, offset, share, 1)
    scaled_cols = lax.dynamic_slice_in_dim(scaled_slots, offset, share, 1)
    got_input, got_scaled = (
        lax.all_to_all(input_cols, "expert", split_axis=0, concat_axis=0, tiled=True),
        lax.all_to_all(scaled_cols, "expert", split_axis=0, concat_axis=0, tiled=True),
    )
    all_inputs, all_scaled = (
        lax.all_gather(got_input, "dp", axis=1, tiled=True),
        lax.all_gather(got_scaled, "dp", axis=1, tiled=True),
    )
    pre_act = jnp.dot(all_inputs, w_pair, preferred_element_type=jnp.float32)
    pre_gate = pre_act[:, :hidden_part]
    pre_up = pre_act[:, hidden_part:]
    activated, slope = silu_parts(pre_gate)
    hidden = (activated * pre_up).astype(jnp.bfloat16)
    hidden_grad = lax.dot_general(
        all_scaled, down_rows, contract_last, preferred_element_type=jnp.float32
    )
    down_grad = lax.dot_general(
        hidden, all_scaled, contract_first, preferred_element_type=jnp.float32
    )
    up_grad = (hidden_grad * activated).astype(jnp.bfloat16)
    gate_grad = (hidden_grad * pre_up * slope).astype(jnp.bfloat16)
    pair_grad = jnp.concatenate([gate_grad, up_grad], axis=1)
    weight_grad = lax.dot_general(
        all_inputs, pair_grad, contract_first, preferred_element_type=jnp.float32
    )
    terms = lax.dot_general(pair_grad, w_pair, contract_last, preferred_element_type=jnp.float32)
    weight_grad, down_grad, terms = (weight_grad, down_grad, terms)
    summed = lax.psum_scatter(terms.astype(jnp.bfloat16), "dp", scatter_dimension=1, tiled=True)
    returned_rows = lax.all_to_all(summed, "expert", split_axis=0, concat_axis=0, tiled=True)
    token_cols = lax.dot_general(
        assign, returned_rows, contract_first, preferred_element_type=jnp.float32
    ).astype(jnp.bfloat16)
    grad_tokens = lax.all_gather(token_cols, "dp", axis=1, tiled=True)
    gate_wgrad = weight_grad[:, :hidden_part].astype(jnp.bfloat16)
    up_wgrad = weight_grad[:, hidden_part:].astype(jnp.bfloat16)
    return (grad_tokens, gate_wgrad[None], up_wgrad[None], down_grad.astype(jnp.bfloat16)[None])


SMALL = 1000
HBM = pltpu.MemorySpace.HBM


def call(body, outs, operands, flops, limit, scratch=(), far=0, aliases=None, out_space=VMEM):
    nbytes = sum(a.size * a.dtype.itemsize for a in operands)
    nbytes += sum(o.size * o.dtype.itemsize for o in outs)
    return pl.pallas_call(
        body,
        out_shape=outs,
        in_specs=[pl.BlockSpec(memory_space=HBM)] * far
        + [pl.BlockSpec(memory_space=VMEM)] * (len(operands) - far),
        out_specs=[pl.BlockSpec(memory_space=out_space)] * len(outs),
        scratch_shapes=list(scratch),
        input_output_aliases=aliases or {},
        compiler_params=pltpu.CompilerParams(vmem_limit_bytes=limit << 20),
        cost_estimate=pl.CostEstimate(flops=flops, bytes_accessed=nbytes, transcendentals=0),
    )(*[pltpu.with_memory_space_constraint(a, HBM) for a in operands[:far]], *operands[far:])


def shape(*dims, dtype=BF16):
    return jax.ShapeDtypeStruct(dims, dtype)


def cols(block, width):
    return pl.ds(pl.multiple_of(block * width, width), width)


def column(row):
    return jnp.transpose(jnp.broadcast_to(row, (128, row.shape[1])))[:, 0:1]


def start_copies(sems, *pairs):
    copies = [pltpu.make_async_copy(src, dst, sems.at[j]) for j, (src, dst) in enumerate(pairs)]
    for copy in copies:
        copy.start()
    return copies


def dispatch_kernel(
    capacity, share, ids_far, prob_far, tok, grad, send1, send2, send3, assign,
    ids, prob, tok_part, grad_part, sems,
):
    here = lax.axis_index("expert")
    piece = cols(lax.axis_index("dp"), share)
    ids_copy, prob_copy, tok_copy, grad_copy = start_copies(
        sems,
        (ids_far, ids),
        (prob_far, prob),
        (tok.at[:, piece], tok_part),
        (grad.at[:, piece], grad_part),
    )
    ids_copy.wait()
    count = tok.shape[0]
    places = assign.shape[0]
    relative = jnp.bitwise_xor(ids[...], here)
    expert = lax.broadcasted_iota(jnp.int32, (8, count), 0)
    hit = (relative == expert).astype(F32)
    row = lax.broadcasted_iota(jnp.int32, (count, count), 0)
    col = lax.broadcasted_iota(jnp.int32, (count, count), 1)
    earlier = (row < col).astype(F32).astype(BF16)
    before = jnp.dot(hit.astype(BF16), earlier, preferred_element_type=F32)
    slot = jnp.sum(before * hit, axis=0, keepdims=True).astype(jnp.int32)
    target = relative * capacity + slot
    spots = lax.broadcasted_iota(jnp.int32, (places, count), 0)
    assign[...] = (target == spots).astype(F32).astype(BF16)
    prob_copy.wait()
    weight = column(prob[...])
    tok_copy.wait()
    for k, ref in ((1, send1), (3, send3), (2, send2)):
        pick = assign[k * capacity : (k + 1) * capacity]
        ref[:capacity] = jnp.dot(pick, tok_part[...], preferred_element_type=F32).astype(BF16)
    grad_copy.wait()
    y_part = (weight * grad_part[...].astype(F32)).astype(BF16)
    for k, ref in ((1, send1), (3, send3), (2, send2)):
        pick = assign[k * capacity : (k + 1) * capacity]
        ref[capacity:] = jnp.dot(pick, y_part, preferred_element_type=F32).astype(BF16)


def block_order():
    core = jnp.bitwise_and(lax.axis_index("dp"), 1)
    first = 2 + 2 * core
    second = 4 - 2 * core
    return (0, first, second, 6), (1, second + 1, first + 1, 7)


def expert_math(share, rows, spot, shared, terms, weights, ready=(lambda: None,) * 3):
    x_all, y_all, hidden, gate_grad, up_grad = shared
    even, odd = terms
    w_gate, w_up, w_down = weights
    block = lax.axis_index("dp")
    ready[0]()
    pre_gate = jnp.dot(x_all[rows], w_gate[...], preferred_element_type=F32)
    ready[1]()
    pre_up = jnp.dot(x_all[rows], w_up[...], preferred_element_type=F32)
    ready[2]()
    hidden_grad = lax.dot_general(y_all[rows], w_down[...], LAST, preferred_element_type=F32)
    activated, slope = silu_parts(pre_gate)
    hidden[rows] = (activated * pre_up).astype(BF16)
    gate_part = (hidden_grad * pre_up * slope).astype(BF16)
    up_part = (hidden_grad * activated).astype(BF16)
    gate_grad[rows] = gate_part
    up_grad[rows] = up_part
    mine, across = block_order()
    for out, order in ((odd, across), (even, mine)):
        for j, k in enumerate(order):
            piece = cols(jnp.bitwise_xor(block, k), share)
            term = lax.dot_general(gate_part, w_gate[piece, :], LAST, preferred_element_type=F32)
            term += lax.dot_general(up_part, w_up[piece, :], LAST, preferred_element_type=F32)
            out[j, spot] = term.astype(BF16)


def own_kernel(
    share, spot, prob_far, tok_far, grad_far, gate_far, up_far, down_far, assign,
    x_all, y_all, hidden, gate_grad, up_grad, even, odd, w_gate, w_up, w_down,
    prob, tok, grad, sems,
):
    prob_copy, tok_copy, grad_copy, *weight_copies = start_copies(
        sems,
        (prob_far, prob),
        (tok_far, tok),
        (grad_far, grad),
        (gate_far, w_gate),
        (up_far, w_up),
        (down_far, w_down),
    )
    own = assign[: spot.stop - spot.start]
    tok_copy.wait()
    x_all[spot] = jnp.dot(own, tok[...], preferred_element_type=F32).astype(BF16)
    prob_copy.wait()
    grad_copy.wait()
    scaled = (column(prob[...]) * grad[...].astype(F32)).astype(BF16)
    y_all[spot] = jnp.dot(own, scaled, preferred_element_type=F32).astype(BF16)
    expert_math(
        share, spot, spot, (x_all, y_all, hidden, gate_grad, up_grad), (even, odd),
        (w_gate, w_up, w_down), [copy.wait for copy in weight_copies],
    )


def chunk_kernel(share, rows, spot, pieces, extra, *refs):
    blocks = list(refs[:4])
    for ref in refs[4 : 4 + pieces]:
        blocks += parts_of(ref, 4 // pieces)
    rest = refs[4 + pieces :]
    weights = rest[:3]
    outs = rest[3 + extra :]
    x_all, y_all = outs[:2]
    block = lax.axis_index("dp")
    mine, across = block_order()
    for k, ref in zip(mine + across, blocks):
        x_part, y_part = halves_of(ref)
        piece = cols(jnp.bitwise_xor(block, k), share)
        x_all[rows, piece] = x_part[...]
        y_all[rows, piece] = y_part[...]
    expert_math(share, rows, spot, outs[:5], outs[5:7], weights)


def wgrad_kernel(left, right, out, tile, sems):
    blocks = tile.shape[0]
    rows = tile.shape[1]
    copies = []
    for j in range(blocks):
        part = left[:, j * rows : (j + 1) * rows]
        total = lax.dot_general(part, right[...], FIRST, preferred_element_type=F32)
        tile[j] = total.astype(BF16)
        copy = pltpu.make_async_copy(tile.at[j], out.at[pl.ds(j * rows, rows)], sems.at[j])
        copy.start()
        copies.append(copy)
    for copy in copies:
        copy.wait()


def combine_kernel(assign, r0, r1, r2, r3, out, rows):
    capacity = r0.shape[0]
    for k, ref in enumerate((r0, r1, r2, r3)):
        rows[k * capacity : (k + 1) * capacity] = ref[...]
    out[...] = lax.dot_general(assign[...], rows[...], FIRST, preferred_element_type=F32).astype(BF16)


def place_kernel(share, *refs):
    out, sems = refs[-2:]
    block = lax.axis_index("dp")
    mine, across = block_order()
    pieces = [cols(jnp.bitwise_xor(block, k), share) for k in mine + across]
    blocks = list(refs[:4]) + parts_of(refs[4], 4)
    for copy in start_copies(sems, *[(b, out.at[:, p]) for b, p in zip(blocks, pieces)]):
        copy.wait()


def fence(*arrays):
    return lax.optimization_barrier(arrays)


def swap(array, axis, distance):
    size = lax.axis_size(axis)
    return lax.ppermute(array, axis, [(i, i ^ distance) for i in range(size)])


def halves_of(ref):
    half = ref.shape[0] // 2
    return (ref.at[pl.ds(0, half)], ref.at[pl.ds(half, half)])


def parts_of(ref, count):
    rows = ref.shape[0] // count
    return [ref.at[pl.ds(j * rows, rows)] for j in range(count)]


def swap_first(array):
    return lax.ppermute(array, "dp", [(i, i ^ (4 if i % 2 else 2)) for i in range(8)])


def swap_second(array):
    return lax.ppermute(array, "dp", [(i, i ^ (2 if i % 2 else 4)) for i in range(8)])


def core_pairs(even, other):
    return [(even[j].astype(F32) + other[j].astype(F32)).astype(BF16) for j in range(4)]


def total_of(parts):
    return sum(part.astype(F32) for part in parts).astype(BF16)


def per_device_blocks(tokens, grad_out, expert_ids, gate_prob, w_gate, w_up, w_down):
    count, width = tokens.shape
    experts = lax.axis_size("expert")
    share = width // lax.axis_size("dp")
    capacity = max(2, (5 * count + 2 * experts - 1) // (2 * experts))
    hidden_part = w_gate.shape[2]
    weights = (w_gate[0], w_up[0], w_down[0])

    ids = expert_ids.T
    prob = gate_prob.T
    send1, send2, send3, assign = call(
        functools.partial(dispatch_kernel, capacity, share),
        [shape(2 * capacity, share)] * 3 + [shape(experts * capacity, count)],
        (ids, prob, tokens, grad_out),
        SMALL,
        8,
        [pltpu.VMEM((1, count), jnp.int32), pltpu.VMEM((1, count), F32)]
        + [pltpu.VMEM((count, share), BF16)] * 2
        + [pltpu.SemaphoreType.DMA((4,))],
        far=4,
    )
    got1 = swap(send1, "expert", 1)
    got3 = swap(send3, "expert", 3)
    total_rows = experts * capacity
    chunk_a = slice(0, 2 * capacity)
    chunk_own = slice(2 * capacity, 3 * capacity)
    chunk_b = slice(3 * capacity, 4 * capacity)
    shared = [shape(total_rows, width)] * 2 + [shape(total_rows, hidden_part)] * 3
    terms_a = [shape(4, 3 * capacity, share)] * 2
    terms_b = [shape(4, capacity, share)] * 2
    own_out = call(
        functools.partial(own_kernel, share, chunk_own),
        shared + terms_a + [shape(*w.shape) for w in weights],
        (prob, tokens, grad_out) + weights + (assign,),
        SMALL,
        20,
        [pltpu.VMEM((1, count), F32)]
        + [pltpu.VMEM((count, width), BF16)] * 2
        + [pltpu.SemaphoreType.DMA((6,))],
        far=6,
    )
    send2, *own_out = fence(send2, *own_out)
    block_b = swap(send2, "expert", 2)
    got1, got3, *own_out = fence(got1, got3, *own_out)
    weights = tuple(own_out[7:])

    block_a = jnp.concatenate(
        [got1[:capacity], got3[:capacity], got1[capacity:], got3[capacity:]], axis=0
    )
    first_a = swap_first(block_a)
    second_a = swap_second(block_a)
    first_a, block_b = fence(first_a, block_b)
    third_a = swap_second(first_a)
    first_b = swap_first(block_b)
    second_b = swap_second(block_b)
    second_a, third_a, first_b = fence(second_a, third_a, first_b)

    across_a = swap(jnp.concatenate([block_a, first_a, second_a, third_a]), "dp", 1)
    third_b = swap_second(first_b)
    early_b = swap(jnp.concatenate([block_b, first_b]), "dp", 1)
    out_a = call(
        functools.partial(chunk_kernel, share, chunk_a, chunk_a, 1, 7),
        shared + terms_a,
        (block_a, first_a, second_a, third_a, across_a) + weights + tuple(own_out[:7]),
        SMALL,
        16,
        aliases={8 + j: j for j in range(7)},
    )
    second_b, third_b, early_b, *out_a = fence(second_b, third_b, early_b, *out_a)

    later_b, *out_a = fence(swap(jnp.concatenate([second_b, third_b]), "dp", 1), *out_a)
    other_a = swap(out_a[6], "dp", 1)
    out_b = call(
        functools.partial(chunk_kernel, share, chunk_b, slice(0, capacity), 2, 5),
        shared + terms_b,
        (block_b, first_b, second_b, third_b, early_b, later_b) + weights + tuple(out_a[:5]),
        SMALL,
        16,
        aliases={9 + j: j for j in range(5)},
    )
    other_a, *out_b = fence(other_a, *out_b)
    x_all, y_all, hidden, gate_grad, up_grad = out_b[:5]
    (other_b,) = fence(swap(out_b[6], "dp", 1))

    def wgrad(left, right):
        blocks = 4
        scratch = [
            pltpu.VMEM((blocks, left.shape[1] // blocks, right.shape[1]), BF16),
            pltpu.SemaphoreType.DMA((blocks,)),
        ]
        (out,) = call(
            wgrad_kernel,
            [shape(left.shape[1], right.shape[1])],
            (left, right),
            SMALL,
            16,
            scratch,
            out_space=HBM,
        )
        return out

    pairs_a = core_pairs(out_a[5], other_a)
    pairs_b = core_pairs(out_b[5], other_b)
    pairs = [jnp.concatenate([pairs_a[j], pairs_b[j]]) for j in range(4)]
    relay = swap_second(pairs[3])
    late = swap_second(pairs[2])
    (relay,) = fence(relay)
    last = swap_first(total_of([pairs[1], relay]))
    up_wgrad = wgrad(x_all, up_grad)
    last, late, up_wgrad, x_all = fence(last, late, up_wgrad, x_all)
    summed = total_of([pairs[0], last, late])
    ret0 = summed[chunk_own]
    ret3 = swap(summed[capacity : 2 * capacity], "expert", 3)
    ret1 = swap(summed[:capacity], "expert", 1)
    ret2 = swap(summed[chunk_b], "expert", 2)
    gate_wgrad = wgrad(x_all, gate_grad)
    ret1, ret2, ret3, gate_wgrad = fence(ret1, ret2, ret3, gate_wgrad)
    (token_cols,) = call(
        combine_kernel,
        [shape(count, share)],
        (assign, ret0, ret1, ret2, ret3),
        SMALL,
        8,
        [pltpu.VMEM((experts * capacity, share), BF16)],
    )
    sixth = swap(token_cols, "dp", 6)
    first = swap_first(token_cols)
    second = swap_second(token_cols)
    down_wgrad = wgrad(hidden, y_all)
    first, second, sixth, down_wgrad = fence(first, second, sixth, down_wgrad)
    across = swap(jnp.concatenate([token_cols, first, second, sixth]), "dp", 1)
    (grad_tokens,) = call(
        functools.partial(place_kernel, share),
        [shape(count, width)],
        (token_cols, first, second, sixth, across),
        SMALL,
        8,
        [pltpu.SemaphoreType.DMA((8,))],
        out_space=HBM,
    )
    return (grad_tokens, gate_wgrad[None], up_wgrad[None], down_wgrad[None])


def solution(mesh):
    placed = (
        P("expert", None),
        P("expert", None),
        P("expert", None),
        P("expert", None),
        P("expert", None, "dp"),
        P("expert", None, "dp"),
        P("expert", "dp", None),
    )
    fits = mesh.shape["dp"] == 8 and mesh.shape["expert"] == 4
    return jax.shard_map(
        per_device_blocks if fits else per_device_any,
        mesh=mesh,
        in_specs=placed,
        out_specs=(
            P("expert", None),
            P("expert", None, "dp"),
            P("expert", None, "dp"),
            P("expert", "dp", None),
        ),
        check_vma=False,
    )
```

```python
import functools
import jax
import jax.numpy as jnp
from jax import lax
from jax.experimental import pallas as pl
from jax.experimental.pallas import tpu as pltpu
from jax.sharding import PartitionSpec as P

BF16 = jnp.bfloat16
F32 = jnp.float32
LAST = (((1,), (1,)), ((), ()))
FIRST = (((0,), (0,)), ((), ()))
VMEM = pltpu.MemorySpace.VMEM


def silu_parts(pre_gate):
    sigma = jax.nn.sigmoid(pre_gate)
    return (pre_gate * sigma, sigma * (1.0 + pre_gate * (1.0 - sigma)))


def per_device_any(tokens, grad_out, expert_ids, gate_prob, w_gate, w_up, w_down):
    expert_count = lax.axis_size("expert")
    replica_count = lax.axis_size("dp")
    tok_count = tokens.shape[0]
    width_all = tokens.shape[1]
    capacity = max(2, (5 * tok_count + 2 * expert_count - 1) // (2 * expert_count))
    routed = expert_ids[:, 0]
    one_hot = (routed[:, None] == jnp.arange(expert_count, dtype=jnp.int32)[None, :]).astype(
        jnp.int32
    )
    slot_index = jnp.sum((jnp.cumsum(one_hot, axis=0) - one_hot) * one_hot, axis=1)
    target = routed * capacity + slot_index
    assign = (
        target[None, :] == jnp.arange(expert_count * capacity, dtype=jnp.int32)[:, None]
    ).astype(jnp.bfloat16)
    scaled = (gate_prob * grad_out.astype(jnp.float32)).astype(jnp.bfloat16)
    input_slots = jnp.dot(assign, tokens, preferred_element_type=jnp.float32).astype(jnp.bfloat16)
    scaled_slots = jnp.dot(assign, scaled, preferred_element_type=jnp.float32).astype(jnp.bfloat16)
    hidden_part = w_gate.shape[2]
    w_pair = jnp.concatenate([w_gate[0], w_up[0]], axis=1)
    down_rows = w_down[0]
    contract_last = (((1,), (1,)), ((), ()))
    contract_first = (((0,), (0,)), ((), ()))
    share = width_all // replica_count
    offset = lax.axis_index("dp") * share
    input_cols = lax.dynamic_slice_in_dim(input_slots, offset, share, 1)
    scaled_cols = lax.dynamic_slice_in_dim(scaled_slots, offset, share, 1)
    got_input, got_scaled = (
        lax.all_to_all(input_cols, "expert", split_axis=0, concat_axis=0, tiled=True),
        lax.all_to_all(scaled_cols, "expert", split_axis=0, concat_axis=0, tiled=True),
    )
    all_inputs, all_scaled = (
        lax.all_gather(got_input, "dp", axis=1, tiled=True),
        lax.all_gather(got_scaled, "dp", axis=1, tiled=True),
    )
    pre_act = jnp.dot(all_inputs, w_pair, preferred_element_type=jnp.float32)
    pre_gate = pre_act[:, :hidden_part]
    pre_up = pre_act[:, hidden_part:]
    activated, slope = silu_parts(pre_gate)
    hidden = (activated * pre_up).astype(jnp.bfloat16)
    hidden_grad = lax.dot_general(
        all_scaled, down_rows, contract_last, preferred_element_type=jnp.float32
    )
    down_grad = lax.dot_general(
        hidden, all_scaled, contract_first, preferred_element_type=jnp.float32
    )
    up_grad = (hidden_grad * activated).astype(jnp.bfloat16)
    gate_grad = (hidden_grad * pre_up * slope).astype(jnp.bfloat16)
    pair_grad = jnp.concatenate([gate_grad, up_grad], axis=1)
    weight_grad = lax.dot_general(
        all_inputs, pair_grad, contract_first, preferred_element_type=jnp.float32
    )
    terms = lax.dot_general(pair_grad, w_pair, contract_last, preferred_element_type=jnp.float32)
    weight_grad, down_grad, terms = (weight_grad, down_grad, terms)
    summed = lax.psum_scatter(terms.astype(jnp.bfloat16), "dp", scatter_dimension=1, tiled=True)
    returned_rows = lax.all_to_all(summed, "expert", split_axis=0, concat_axis=0, tiled=True)
    token_cols = lax.dot_general(
        assign, returned_rows, contract_first, preferred_element_type=jnp.float32
    ).astype(jnp.bfloat16)
    grad_tokens = lax.all_gather(token_cols, "dp", axis=1, tiled=True)
    gate_wgrad = weight_grad[:, :hidden_part].astype(jnp.bfloat16)
    up_wgrad = weight_grad[:, hidden_part:].astype(jnp.bfloat16)
    return (grad_tokens, gate_wgrad[None], up_wgrad[None], down_grad.astype(jnp.bfloat16)[None])


SMALL = 1000
HBM = pltpu.MemorySpace.HBM


def call(body, outs, operands, flops, limit, scratch=(), far=0, aliases=None, out_space=VMEM):
    nbytes = sum(a.size * a.dtype.itemsize for a in operands)
    nbytes += sum(o.size * o.dtype.itemsize for o in outs)
    return pl.pallas_call(
        body,
        out_shape=outs,
        in_specs=[pl.BlockSpec(memory_space=HBM)] * far
        + [pl.BlockSpec(memory_space=VMEM)] * (len(operands) - far),
        out_specs=[pl.BlockSpec(memory_space=out_space)] * len(outs),
        scratch_shapes=list(scratch),
        input_output_aliases=aliases or {},
        compiler_params=pltpu.CompilerParams(vmem_limit_bytes=limit << 20),
        cost_estimate=pl.CostEstimate(flops=flops, bytes_accessed=nbytes, transcendentals=0),
    )(*[pltpu.with_memory_space_constraint(a, HBM) for a in operands[:far]], *operands[far:])


def shape(*dims, dtype=BF16):
    return jax.ShapeDtypeStruct(dims, dtype)


def cols(block, width):
    return pl.ds(pl.multiple_of(block * width, width), width)


def column(row):
    return jnp.transpose(jnp.broadcast_to(row, (128, row.shape[1])))[:, 0:1]


def start_copies(sems, *pairs):
    copies = [pltpu.make_async_copy(src, dst, sems.at[j]) for j, (src, dst) in enumerate(pairs)]
    for copy in copies:
        copy.start()
    return copies


def dispatch_kernel(
    capacity, share, ids_far, prob_far, tok, grad, send1, send2, send3, assign,
    ids, prob, tok_part, grad_part, sems,
):
    here = lax.axis_index("expert")
    piece = cols(lax.axis_index("dp"), share)
    ids_copy, prob_copy, tok_copy, grad_copy = start_copies(
        sems,
        (ids_far, ids),
        (prob_far, prob),
        (tok.at[:, piece], tok_part),
        (grad.at[:, piece], grad_part),
    )
    ids_copy.wait()
    count = tok.shape[0]
    places = assign.shape[0]
    relative = jnp.bitwise_xor(ids[...], here)
    expert = lax.broadcasted_iota(jnp.int32, (8, count), 0)
    hit = (relative == expert).astype(F32)
    row = lax.broadcasted_iota(jnp.int32, (count, count), 0)
    col = lax.broadcasted_iota(jnp.int32, (count, count), 1)
    earlier = (row < col).astype(F32).astype(BF16)
    before = jnp.dot(hit.astype(BF16), earlier, preferred_element_type=F32)
    slot = jnp.sum(before * hit, axis=0, keepdims=True).astype(jnp.int32)
    target = relative * capacity + slot
    spots = lax.broadcasted_iota(jnp.int32, (places, count), 0)
    assign[...] = (target == spots).astype(F32).astype(BF16)
    prob_copy.wait()
    weight = column(prob[...])
    tok_copy.wait()
    for k, ref in ((1, send1), (3, send3), (2, send2)):
        pick = assign[k * capacity : (k + 1) * capacity]
        ref[:capacity] = jnp.dot(pick, tok_part[...], preferred_element_type=F32).astype(BF16)
    grad_copy.wait()
    y_part = (weight * grad_part[...].astype(F32)).astype(BF16)
    for k, ref in ((1, send1), (3, send3), (2, send2)):
        pick = assign[k * capacity : (k + 1) * capacity]
        ref[capacity:] = jnp.dot(pick, y_part, preferred_element_type=F32).astype(BF16)


def block_order():
    core = jnp.bitwise_and(lax.axis_index("dp"), 1)
    first = 2 + 2 * core
    second = 4 - 2 * core
    return (0, first, second, 6), (1, second + 1, first + 1, 7)


def forward_sums(parts, weights, ready=(lambda: None,) * 3):
    sums = []
    for weight, wait in zip(weights, ready):
        wait()
        total = 0.0
        for x_part, y_part, piece in parts:
            if weight is weights[2]:
                total += lax.dot_general(
                    y_part, weight[:, piece], LAST, preferred_element_type=F32
                )
            else:
                total += jnp.dot(x_part, weight[piece, :], preferred_element_type=F32)
        sums.append(total)
    return sums


def gradients(sums, hidden, gate_grad, up_grad, rows):
    pre_gate, pre_up, hidden_grad = sums
    activated, slope = silu_parts(pre_gate)
    hidden[rows] = (activated * pre_up).astype(BF16)
    gate_grad[rows] = (hidden_grad * pre_up * slope).astype(BF16)
    up_grad[rows] = (hidden_grad * activated).astype(BF16)


def input_terms(share, order, gate_part, up_part, w_gate, w_up, out, spot):
    block = lax.axis_index("dp")
    for j, k in enumerate(order):
        piece = cols(jnp.bitwise_xor(block, k), share)
        term = lax.dot_general(gate_part, w_gate[piece, :], LAST, preferred_element_type=F32)
        term += lax.dot_general(up_part, w_up[piece, :], LAST, preferred_element_type=F32)
        out[j, spot] = term.astype(BF16)


def expert_math(share, rows, spot, shared, terms, weights, ready=(lambda: None,) * 3):
    x_all, y_all, hidden, gate_grad, up_grad = shared
    sums = forward_sums([(x_all[rows], y_all[rows], slice(None))], weights, ready)
    gradients(sums, hidden, gate_grad, up_grad, rows)
    mine, across = block_order()
    for out, order in zip(terms, (mine, across)):
        input_terms(share, order, gate_grad[rows], up_grad[rows], weights[0], weights[1], out, spot)


def early_kernel(share, *refs):
    blocks = list(refs[:4]) + parts_of(refs[4], 2)
    weights, outs = refs[5:8], refs[8:]
    block = lax.axis_index("dp")
    mine, across = block_order()
    parts = []
    for k, ref in zip(mine + across[:2], blocks):
        x_part, y_part = halves_of(ref)
        parts.append((x_part[...], y_part[...], cols(jnp.bitwise_xor(block, k), share)))
    for out, total in zip(outs, forward_sums(parts, weights)):
        out[...] = total


def late_kernel(share, rows, *refs):
    blocks = list(refs[:4]) + parts_of(refs[4], 2) + parts_of(refs[5], 2)
    early, weights = refs[6:9], refs[9:12]
    x_all, y_all, hidden, gate_grad, up_grad, odd = refs[17:]
    block = lax.axis_index("dp")
    mine, across = block_order()
    parts = []
    for k, ref in zip(mine + across, blocks):
        x_part, y_part = halves_of(ref)
        piece = cols(jnp.bitwise_xor(block, k), share)
        x_all[rows, piece] = x_part[...]
        y_all[rows, piece] = y_part[...]
        parts.append((x_part, y_part, piece))
    parts = [(x_part[...], y_part[...], piece) for x_part, y_part, piece in parts[6:]]
    sums = [total + part[...] for total, part in zip(forward_sums(parts, weights), early)]
    gradients(sums, hidden, gate_grad, up_grad, rows)
    input_terms(
        share, across, gate_grad[rows], up_grad[rows], weights[0], weights[1], odd, slice(None)
    )


def even_kernel(share, rows, gate_grad, up_grad, w_gate, w_up, even):
    mine, _ = block_order()
    input_terms(share, mine, gate_grad[rows], up_grad[rows], w_gate, w_up, even, slice(None))


def own_kernel(
    share, spot, prob_far, tok_far, grad_far, gate_far, up_far, down_far, assign,
    x_all, y_all, hidden, gate_grad, up_grad, even, odd, w_gate, w_up, w_down,
    prob, tok, grad, sems,
):
    prob_copy, tok_copy, grad_copy, *weight_copies = start_copies(
        sems,
        (prob_far, prob),
        (tok_far, tok),
        (grad_far, grad),
        (gate_far, w_gate),
        (up_far, w_up),
        (down_far, w_down),
    )
    own = assign[: spot.stop - spot.start]
    tok_copy.wait()
    x_all[spot] = jnp.dot(own, tok[...], preferred_element_type=F32).astype(BF16)
    prob_copy.wait()
    grad_copy.wait()
    scaled = (column(prob[...]) * grad[...].astype(F32)).astype(BF16)
    y_all[spot] = jnp.dot(own, scaled, preferred_element_type=F32).astype(BF16)
    expert_math(
        share, spot, spot, (x_all, y_all, hidden, gate_grad, up_grad), (even, odd),
        (w_gate, w_up, w_down), [copy.wait for copy in weight_copies],
    )


def chunk_kernel(share, rows, spot, pieces, extra, *refs):
    blocks = list(refs[:4])
    for ref in refs[4 : 4 + pieces]:
        blocks += parts_of(ref, 4 // pieces)
    rest = refs[4 + pieces :]
    weights = rest[:3]
    outs = rest[3 + extra :]
    x_all, y_all = outs[:2]
    block = lax.axis_index("dp")
    mine, across = block_order()
    for k, ref in zip(mine + across, blocks):
        x_part, y_part = halves_of(ref)
        piece = cols(jnp.bitwise_xor(block, k), share)
        x_all[rows, piece] = x_part[...]
        y_all[rows, piece] = y_part[...]
    expert_math(share, rows, spot, outs[:5], outs[5:7], weights)


def wgrad_kernel(left, right, out, tile, sems):
    blocks = tile.shape[0]
    rows = tile.shape[1]
    copies = []
    for j in range(blocks):
        part = left[:, j * rows : (j + 1) * rows]
        total = lax.dot_general(part, right[...], FIRST, preferred_element_type=F32)
        tile[j] = total.astype(BF16)
        copy = pltpu.make_async_copy(tile.at[j], out.at[pl.ds(j * rows, rows)], sems.at[j])
        copy.start()
        copies.append(copy)
    for copy in copies:
        copy.wait()


def combine_kernel(assign, r0, r1, r2, r3, out, rows):
    capacity = r0.shape[0]
    for k, ref in enumerate((r0, r1, r2, r3)):
        rows[k * capacity : (k + 1) * capacity] = ref[...]
    out[...] = lax.dot_general(assign[...], rows[...], FIRST, preferred_element_type=F32).astype(BF16)


def place_kernel(share, *refs):
    out, sems = refs[-2:]
    block = lax.axis_index("dp")
    mine, across = block_order()
    pieces = [cols(jnp.bitwise_xor(block, k), share) for k in mine + across]
    blocks = list(refs[:4]) + parts_of(refs[4], 4)
    for copy in start_copies(sems, *[(b, out.at[:, p]) for b, p in zip(blocks, pieces)]):
        copy.wait()


def fence(*arrays):
    return lax.optimization_barrier(arrays)


def swap(array, axis, distance):
    size = lax.axis_size(axis)
    return lax.ppermute(array, axis, [(i, i ^ distance) for i in range(size)])


def halves_of(ref):
    half = ref.shape[0] // 2
    return (ref.at[pl.ds(0, half)], ref.at[pl.ds(half, half)])


def parts_of(ref, count):
    rows = ref.shape[0] // count
    return [ref.at[pl.ds(j * rows, rows)] for j in range(count)]


def swap_first(array):
    return lax.ppermute(array, "dp", [(i, i ^ (4 if i % 2 else 2)) for i in range(8)])


def swap_second(array):
    return lax.ppermute(array, "dp", [(i, i ^ (2 if i % 2 else 4)) for i in range(8)])


def core_pairs(even, other):
    return [(even[j].astype(F32) + other[j].astype(F32)).astype(BF16) for j in range(4)]


def total_of(parts):
    return sum(part.astype(F32) for part in parts).astype(BF16)


def per_device_blocks(tokens, grad_out, expert_ids, gate_prob, w_gate, w_up, w_down):
    count, width = tokens.shape
    experts = lax.axis_size("expert")
    share = width // lax.axis_size("dp")
    capacity = max(2, (5 * count + 2 * experts - 1) // (2 * experts))
    hidden_part = w_gate.shape[2]
    weights = (w_gate[0], w_up[0], w_down[0])

    ids = expert_ids.T
    prob = gate_prob.T
    send1, send2, send3, assign = call(
        functools.partial(dispatch_kernel, capacity, share),
        [shape(2 * capacity, share)] * 3 + [shape(experts * capacity, count)],
        (ids, prob, tokens, grad_out),
        SMALL,
        8,
        [pltpu.VMEM((1, count), jnp.int32), pltpu.VMEM((1, count), F32)]
        + [pltpu.VMEM((count, share), BF16)] * 2
        + [pltpu.SemaphoreType.DMA((4,))],
        far=4,
    )
    got1 = swap(send1, "expert", 1)
    got3 = swap(send3, "expert", 3)
    total_rows = experts * capacity
    chunk_a = slice(0, 2 * capacity)
    chunk_own = slice(2 * capacity, 3 * capacity)
    chunk_b = slice(3 * capacity, 4 * capacity)
    shared = [shape(total_rows, width)] * 2 + [shape(total_rows, hidden_part)] * 3
    terms_a = [shape(4, 3 * capacity, share)] * 2
    terms_b = [shape(4, capacity, share)] * 2
    own_out = call(
        functools.partial(own_kernel, share, chunk_own),
        shared + terms_a + [shape(*w.shape) for w in weights],
        (prob, tokens, grad_out) + weights + (assign,),
        SMALL,
        20,
        [pltpu.VMEM((1, count), F32)]
        + [pltpu.VMEM((count, width), BF16)] * 2
        + [pltpu.SemaphoreType.DMA((6,))],
        far=6,
    )
    send2, *own_out = fence(send2, *own_out)
    block_b = swap(send2, "expert", 2)
    got1, got3, *own_out = fence(got1, got3, *own_out)
    weights = tuple(own_out[7:])

    block_a = jnp.concatenate(
        [got1[:capacity], got3[:capacity], got1[capacity:], got3[capacity:]], axis=0
    )
    first_a = swap_first(block_a)
    second_a = swap_second(block_a)
    first_a, block_b = fence(first_a, block_b)
    third_a = swap_second(first_a)
    first_b = swap_first(block_b)
    second_b = swap_second(block_b)
    second_a, third_a, first_b = fence(second_a, third_a, first_b)

    across_a = swap(jnp.concatenate([block_a, first_a, second_a, third_a]), "dp", 1)
    third_b = swap_second(first_b)
    early_b = swap(jnp.concatenate([block_b, first_b]), "dp", 1)
    out_a = call(
        functools.partial(chunk_kernel, share, chunk_a, chunk_a, 1, 7),
        shared + terms_a,
        (block_a, first_a, second_a, third_a, across_a) + weights + tuple(own_out[:7]),
        SMALL,
        16,
        aliases={8 + j: j for j in range(7)},
    )
    second_b, third_b, early_b, *out_a = fence(second_b, third_b, early_b, *out_a)

    partial = call(
        functools.partial(early_kernel, share),
        [shape(capacity, hidden_part, dtype=F32)] * 3,
        (block_b, first_b, second_b, third_b, early_b) + weights,
        SMALL,
        16,
    )
    later_b = swap(jnp.concatenate([second_b, third_b]), "dp", 1)
    later_b, *out_a = fence(later_b, *out_a, *partial)
    out_a, partial = out_a[:7], tuple(out_a[7:])
    other_a = swap(out_a[6], "dp", 1)
    out_b = call(
        functools.partial(late_kernel, share, chunk_b),
        shared + terms_b[:1],
        (block_b, first_b, second_b, third_b, early_b, later_b)
        + partial
        + weights
        + tuple(out_a[:5]),
        SMALL,
        16,
        aliases={12 + j: j for j in range(5)},
    )
    other_a, *out_b = fence(other_a, *out_b)
    x_all, y_all, hidden, gate_grad, up_grad, odd_b = out_b
    (even_b,) = call(
        functools.partial(even_kernel, share, chunk_b),
        terms_b[:1],
        (gate_grad, up_grad) + weights[:2],
        SMALL,
        16,
    )
    other_b, even_b = fence(swap(odd_b, "dp", 1), even_b)

    def wgrad(left, right):
        blocks = 4
        scratch = [
            pltpu.VMEM((blocks, left.shape[1] // blocks, right.shape[1]), BF16),
            pltpu.SemaphoreType.DMA((blocks,)),
        ]
        (out,) = call(
            wgrad_kernel,
            [shape(left.shape[1], right.shape[1])],
            (left, right),
            SMALL,
            16,
            scratch,
            out_space=HBM,
        )
        return out

    pairs_a = core_pairs(out_a[5], other_a)
    pairs_b = core_pairs(even_b, other_b)
    pairs = [jnp.concatenate([pairs_a[j], pairs_b[j]]) for j in range(4)]
    relay = swap_second(pairs[3])
    late = swap_second(pairs[2])
    (relay,) = fence(relay)
    last = swap_first(total_of([pairs[1], relay]))
    up_wgrad = wgrad(x_all, up_grad)
    last, late, up_wgrad, x_all = fence(last, late, up_wgrad, x_all)
    summed = total_of([pairs[0], last, late])
    ret0 = summed[chunk_own]
    ret3 = swap(summed[capacity : 2 * capacity], "expert", 3)
    ret1 = swap(summed[:capacity], "expert", 1)
    ret2 = swap(summed[chunk_b], "expert", 2)
    gate_wgrad = wgrad(x_all, gate_grad)
    ret1, ret2, ret3, gate_wgrad = fence(ret1, ret2, ret3, gate_wgrad)
    (token_cols,) = call(
        combine_kernel,
        [shape(count, share)],
        (assign, ret0, ret1, ret2, ret3),
        SMALL,
        8,
        [pltpu.VMEM((experts * capacity, share), BF16)],
    )
    sixth = swap(token_cols, "dp", 6)
    first = swap_first(token_cols)
    second = swap_second(token_cols)
    down_wgrad = wgrad(hidden, y_all)
    first, second, sixth, down_wgrad = fence(first, second, sixth, down_wgrad)
    across = swap(jnp.concatenate([token_cols, first, second, sixth]), "dp", 1)
    (grad_tokens,) = call(
        functools.partial(place_kernel, share),
        [shape(count, width)],
        (token_cols, first, second, sixth, across),
        SMALL,
        8,
        [pltpu.SemaphoreType.DMA((8,))],
        out_space=HBM,
    )
    return (grad_tokens, gate_wgrad[None], up_wgrad[None], down_wgrad[None])


def solution(mesh):
    placed = (
        P("expert", None),
        P("expert", None),
        P("expert", None),
        P("expert", None),
        P("expert", None, "dp"),
        P("expert", None, "dp"),
        P("expert", "dp", None),
    )
    fits = mesh.shape["dp"] == 8 and mesh.shape["expert"] == 4
    return jax.shard_map(
        per_device_blocks if fits else per_device_any,
        mesh=mesh,
        in_specs=placed,
        out_specs=(
            P("expert", None),
            P("expert", None, "dp"),
            P("expert", None, "dp"),
            P("expert", "dp", None),
        ),
        check_vma=False,
    )
```

```python
import functools
import jax
import jax.numpy as jnp
from jax import lax
from jax.experimental import pallas as pl
from jax.experimental.pallas import tpu as pltpu
from jax.sharding import PartitionSpec as P

BF16 = jnp.bfloat16
F32 = jnp.float32
LAST = (((1,), (1,)), ((), ()))
FIRST = (((0,), (0,)), ((), ()))
VMEM = pltpu.MemorySpace.VMEM


def silu_parts(pre_gate):
    sigma = jax.nn.sigmoid(pre_gate)
    return (pre_gate * sigma, sigma * (1.0 + pre_gate * (1.0 - sigma)))


def per_device_any(tokens, grad_out, expert_ids, gate_prob, w_gate, w_up, w_down):
    expert_count = lax.axis_size("expert")
    replica_count = lax.axis_size("dp")
    tok_count = tokens.shape[0]
    width_all = tokens.shape[1]
    capacity = max(2, (5 * tok_count + 2 * expert_count - 1) // (2 * expert_count))
    routed = expert_ids[:, 0]
    one_hot = (routed[:, None] == jnp.arange(expert_count, dtype=jnp.int32)[None, :]).astype(
        jnp.int32
    )
    slot_index = jnp.sum((jnp.cumsum(one_hot, axis=0) - one_hot) * one_hot, axis=1)
    target = routed * capacity + slot_index
    assign = (
        target[None, :] == jnp.arange(expert_count * capacity, dtype=jnp.int32)[:, None]
    ).astype(jnp.bfloat16)
    scaled = (gate_prob * grad_out.astype(jnp.float32)).astype(jnp.bfloat16)
    input_slots = jnp.dot(assign, tokens, preferred_element_type=jnp.float32).astype(jnp.bfloat16)
    scaled_slots = jnp.dot(assign, scaled, preferred_element_type=jnp.float32).astype(jnp.bfloat16)
    hidden_part = w_gate.shape[2]
    w_pair = jnp.concatenate([w_gate[0], w_up[0]], axis=1)
    down_rows = w_down[0]
    contract_last = (((1,), (1,)), ((), ()))
    contract_first = (((0,), (0,)), ((), ()))
    share = width_all // replica_count
    offset = lax.axis_index("dp") * share
    input_cols = lax.dynamic_slice_in_dim(input_slots, offset, share, 1)
    scaled_cols = lax.dynamic_slice_in_dim(scaled_slots, offset, share, 1)
    got_input, got_scaled = (
        lax.all_to_all(input_cols, "expert", split_axis=0, concat_axis=0, tiled=True),
        lax.all_to_all(scaled_cols, "expert", split_axis=0, concat_axis=0, tiled=True),
    )
    all_inputs, all_scaled = (
        lax.all_gather(got_input, "dp", axis=1, tiled=True),
        lax.all_gather(got_scaled, "dp", axis=1, tiled=True),
    )
    pre_act = jnp.dot(all_inputs, w_pair, preferred_element_type=jnp.float32)
    pre_gate = pre_act[:, :hidden_part]
    pre_up = pre_act[:, hidden_part:]
    activated, slope = silu_parts(pre_gate)
    hidden = (activated * pre_up).astype(jnp.bfloat16)
    hidden_grad = lax.dot_general(
        all_scaled, down_rows, contract_last, preferred_element_type=jnp.float32
    )
    down_grad = lax.dot_general(
        hidden, all_scaled, contract_first, preferred_element_type=jnp.float32
    )
    up_grad = (hidden_grad * activated).astype(jnp.bfloat16)
    gate_grad = (hidden_grad * pre_up * slope).astype(jnp.bfloat16)
    pair_grad = jnp.concatenate([gate_grad, up_grad], axis=1)
    weight_grad = lax.dot_general(
        all_inputs, pair_grad, contract_first, preferred_element_type=jnp.float32
    )
    terms = lax.dot_general(pair_grad, w_pair, contract_last, preferred_element_type=jnp.float32)
    weight_grad, down_grad, terms = (weight_grad, down_grad, terms)
    summed = lax.psum_scatter(terms.astype(jnp.bfloat16), "dp", scatter_dimension=1, tiled=True)
    returned_rows = lax.all_to_all(summed, "expert", split_axis=0, concat_axis=0, tiled=True)
    token_cols = lax.dot_general(
        assign, returned_rows, contract_first, preferred_element_type=jnp.float32
    ).astype(jnp.bfloat16)
    grad_tokens = lax.all_gather(token_cols, "dp", axis=1, tiled=True)
    gate_wgrad = weight_grad[:, :hidden_part].astype(jnp.bfloat16)
    up_wgrad = weight_grad[:, hidden_part:].astype(jnp.bfloat16)
    return (grad_tokens, gate_wgrad[None], up_wgrad[None], down_grad.astype(jnp.bfloat16)[None])


SMALL = 1000
HBM = pltpu.MemorySpace.HBM


def call(body, outs, operands, flops, limit, scratch=(), far=0, aliases=None, out_space=VMEM):
    nbytes = sum(a.size * a.dtype.itemsize for a in operands)
    nbytes += sum(o.size * o.dtype.itemsize for o in outs)
    return pl.pallas_call(
        body,
        out_shape=outs,
        in_specs=[pl.BlockSpec(memory_space=HBM)] * far
        + [pl.BlockSpec(memory_space=VMEM)] * (len(operands) - far),
        out_specs=[pl.BlockSpec(memory_space=out_space)] * len(outs),
        scratch_shapes=list(scratch),
        input_output_aliases=aliases or {},
        compiler_params=pltpu.CompilerParams(vmem_limit_bytes=limit << 20),
        cost_estimate=pl.CostEstimate(flops=flops, bytes_accessed=nbytes, transcendentals=0),
    )(*[pltpu.with_memory_space_constraint(a, HBM) for a in operands[:far]], *operands[far:])


def shape(*dims, dtype=BF16):
    return jax.ShapeDtypeStruct(dims, dtype)


def cols(block, width):
    return pl.ds(pl.multiple_of(block * width, width), width)


def column(row):
    return jnp.transpose(jnp.broadcast_to(row, (128, row.shape[1])))[:, 0:1]


def start_copies(sems, *pairs):
    copies = [pltpu.make_async_copy(src, dst, sems.at[j]) for j, (src, dst) in enumerate(pairs)]
    for copy in copies:
        copy.start()
    return copies


def dispatch_kernel(
    capacity, share, ids_far, prob_far, tok, grad, send1, send2, send3, assign,
    ids, prob, tok_part, grad_part, sems,
):
    here = lax.axis_index("expert")
    piece = cols(lax.axis_index("dp"), share)
    ids_copy, prob_copy, tok_copy, grad_copy = start_copies(
        sems,
        (ids_far, ids),
        (prob_far, prob),
        (tok.at[:, piece], tok_part),
        (grad.at[:, piece], grad_part),
    )
    count = tok.shape[0]
    places = assign.shape[0]
    row = lax.broadcasted_iota(jnp.int32, (count, count), 0)
    col = lax.broadcasted_iota(jnp.int32, (count, count), 1)
    earlier = (row < col).astype(F32).astype(BF16)
    expert = lax.broadcasted_iota(jnp.int32, (8, count), 0)
    spots = lax.broadcasted_iota(jnp.int32, (places, count), 0)
    ids_copy.wait()
    relative = jnp.bitwise_xor(ids[...], here)
    hit = (relative == expert).astype(F32)
    before = jnp.dot(hit.astype(BF16), earlier, preferred_element_type=F32)
    slot = jnp.sum(before * hit, axis=0, keepdims=True).astype(jnp.int32)
    target = relative * capacity + slot
    chosen = (target == spots).astype(F32).astype(BF16)
    assign[...] = chosen
    prob_copy.wait()
    weight = column(prob[...])
    tok_copy.wait()
    grad_copy.wait()
    y_part = (weight * grad_part[...].astype(F32)).astype(BF16)
    both = jnp.concatenate([tok_part[...], y_part], axis=1)
    for k, ref in ((1, send1), (3, send3), (2, send2)):
        pick = chosen[k * capacity : (k + 1) * capacity]
        rows = jnp.dot(pick, both, preferred_element_type=F32).astype(BF16)
        ref[:capacity] = rows[:, :share]
        ref[capacity:] = rows[:, share:]


def block_order():
    core = jnp.bitwise_and(lax.axis_index("dp"), 1)
    first = 2 + 2 * core
    second = 4 - 2 * core
    return (0, first, second, 6), (1, second + 1, first + 1, 7)


def forward_sums(parts, weights, ready=(lambda: None,) * 3):
    sums = []
    for weight, wait in zip(weights, ready):
        wait()
        total = 0.0
        for x_part, y_part, piece in parts:
            if weight is weights[2]:
                total += lax.dot_general(
                    y_part, weight[:, piece], LAST, preferred_element_type=F32
                )
            else:
                total += jnp.dot(x_part, weight[piece, :], preferred_element_type=F32)
        sums.append(total)
    return sums


def gradients(sums, hidden, gate_grad, up_grad, rows):
    pre_gate, pre_up, hidden_grad = sums
    activated, slope = silu_parts(pre_gate)
    hidden[rows] = (activated * pre_up).astype(BF16)
    gate_grad[rows] = (hidden_grad * pre_up * slope).astype(BF16)
    up_grad[rows] = (hidden_grad * activated).astype(BF16)


def input_terms(share, order, gate_part, up_part, w_gate, w_up, out, spot):
    block = lax.axis_index("dp")
    for j, k in enumerate(order):
        piece = cols(jnp.bitwise_xor(block, k), share)
        term = lax.dot_general(gate_part, w_gate[piece, :], LAST, preferred_element_type=F32)
        term += lax.dot_general(up_part, w_up[piece, :], LAST, preferred_element_type=F32)
        out[j, spot] = term.astype(BF16)


def expert_math(share, rows, spot, shared, terms, weights, ready=(lambda: None,) * 3):
    x_all, y_all, hidden, gate_grad, up_grad = shared
    sums = forward_sums([(x_all[rows], y_all[rows], slice(None))], weights, ready)
    gradients(sums, hidden, gate_grad, up_grad, rows)
    mine, across = block_order()
    for out, order in zip(terms, (mine, across)):
        input_terms(share, order, gate_grad[rows], up_grad[rows], weights[0], weights[1], out, spot)


def early_kernel(share, *refs):
    blocks = parts_of(refs[0], 2) + parts_of(refs[1], 2) + parts_of(refs[2], 2)
    weights, outs = refs[3:6], refs[6:]
    block = lax.axis_index("dp")
    mine, across = block_order()
    parts = []
    for k, ref in zip(mine + across[:2], blocks):
        x_part, y_part = halves_of(ref)
        parts.append((x_part[...], y_part[...], cols(jnp.bitwise_xor(block, k), share)))
    for out, total in zip(outs, forward_sums(parts, weights)):
        out[...] = total


def late_kernel(share, rows, *refs):
    blocks = [part for ref in refs[:4] for part in parts_of(ref, 2)]
    early, weights = refs[4:7], refs[7:10]
    x_all, y_all, hidden, gate_grad, up_grad, odd = refs[15:]
    block = lax.axis_index("dp")
    mine, across = block_order()
    parts = []
    for k, ref in zip(mine + across, blocks):
        x_part, y_part = halves_of(ref)
        piece = cols(jnp.bitwise_xor(block, k), share)
        x_all[rows, piece] = x_part[...]
        y_all[rows, piece] = y_part[...]
        parts.append((x_part, y_part, piece))
    parts = [(x_part[...], y_part[...], piece) for x_part, y_part, piece in parts[6:]]
    sums = [total + part[...] for total, part in zip(forward_sums(parts, weights), early)]
    gradients(sums, hidden, gate_grad, up_grad, rows)
    input_terms(
        share, across, gate_grad[rows], up_grad[rows], weights[0], weights[1], odd, slice(None)
    )


def even_kernel(share, rows, gate_grad, up_grad, w_gate, w_up, even):
    mine, _ = block_order()
    input_terms(share, mine, gate_grad[rows], up_grad[rows], w_gate, w_up, even, slice(None))


def own_kernel(
    share, spot, prob_far, tok_far, grad_far, gate_far, up_far, down_far, assign,
    x_all, y_all, hidden, gate_grad, up_grad, even, odd, w_gate, w_up, w_down,
    prob, tok, grad, sems,
):
    prob_copy, tok_copy, grad_copy, *weight_copies = start_copies(
        sems,
        (prob_far, prob),
        (tok_far, tok),
        (grad_far, grad),
        (gate_far, w_gate),
        (up_far, w_up),
        (down_far, w_down),
    )
    own = assign[: spot.stop - spot.start]
    tok_copy.wait()
    x_all[spot] = jnp.dot(own, tok[...], preferred_element_type=F32).astype(BF16)
    prob_copy.wait()
    grad_copy.wait()
    scaled = (column(prob[...]) * grad[...].astype(F32)).astype(BF16)
    y_all[spot] = jnp.dot(own, scaled, preferred_element_type=F32).astype(BF16)
    expert_math(
        share, spot, spot, (x_all, y_all, hidden, gate_grad, up_grad), (even, odd),
        (w_gate, w_up, w_down), [copy.wait for copy in weight_copies],
    )


def chunk_kernel(share, rows, spot, pieces, extra, *refs):
    blocks = list(refs[:4])
    for ref in refs[4 : 4 + pieces]:
        blocks += parts_of(ref, 4 // pieces)
    rest = refs[4 + pieces :]
    weights = rest[:3]
    outs = rest[3 + extra :]
    x_all, y_all = outs[:2]
    block = lax.axis_index("dp")
    mine, across = block_order()
    for k, ref in zip(mine + across, blocks):
        x_part, y_part = halves_of(ref)
        piece = cols(jnp.bitwise_xor(block, k), share)
        x_all[rows, piece] = x_part[...]
        y_all[rows, piece] = y_part[...]
    expert_math(share, rows, spot, outs[:5], outs[5:7], weights)


def wgrad_kernel(left, right, out, tile, sems):
    blocks = tile.shape[0]
    rows = tile.shape[1]
    copies = []
    for j in range(blocks):
        part = left[:, j * rows : (j + 1) * rows]
        total = lax.dot_general(part, right[...], FIRST, preferred_element_type=F32)
        tile[j] = total.astype(BF16)
        copy = pltpu.make_async_copy(tile.at[j], out.at[pl.ds(j * rows, rows)], sems.at[j])
        copy.start()
        copies.append(copy)
    for copy in copies:
        copy.wait()


def combine_kernel(assign, r0, r1, r2, r3, out, rows):
    capacity = r0.shape[0]
    for k, ref in enumerate((r0, r1, r2, r3)):
        rows[k * capacity : (k + 1) * capacity] = ref[...]
    out[...] = lax.dot_general(assign[...], rows[...], FIRST, preferred_element_type=F32).astype(BF16)


def place_kernel(share, side, count, *refs):
    out, sems = refs[-2:]
    block = lax.axis_index("dp")
    pieces = [cols(jnp.bitwise_xor(block, k), share) for k in block_order()[side]]
    blocks = refs[:4] if count == 4 else parts_of(refs[0], 4)
    for copy in start_copies(sems, *[(b, out.at[:, p]) for b, p in zip(blocks, pieces)]):
        copy.wait()


def fence(*arrays):
    return lax.optimization_barrier(arrays)


def swap(array, axis, distance):
    size = lax.axis_size(axis)
    return lax.ppermute(array, axis, [(i, i ^ distance) for i in range(size)])


def halves_of(ref):
    half = ref.shape[0] // 2
    return (ref.at[pl.ds(0, half)], ref.at[pl.ds(half, half)])


def parts_of(ref, count):
    rows = ref.shape[0] // count
    return [ref.at[pl.ds(j * rows, rows)] for j in range(count)]


def swap_first(array):
    return lax.ppermute(array, "dp", [(i, i ^ (4 if i % 2 else 2)) for i in range(8)])


def swap_second(array):
    return lax.ppermute(array, "dp", [(i, i ^ (2 if i % 2 else 4)) for i in range(8)])


def core_pairs(even, other):
    return [(even[j].astype(F32) + other[j].astype(F32)).astype(BF16) for j in range(4)]


def total_of(parts):
    return sum(part.astype(F32) for part in parts).astype(BF16)


def per_device_blocks(tokens, grad_out, expert_ids, gate_prob, w_gate, w_up, w_down):
    count, width = tokens.shape
    experts = lax.axis_size("expert")
    share = width // lax.axis_size("dp")
    capacity = max(2, (5 * count + 2 * experts - 1) // (2 * experts))
    hidden_part = w_gate.shape[2]
    weights = (w_gate[0], w_up[0], w_down[0])

    ids = expert_ids.T
    prob = gate_prob.T
    send1, send2, send3, assign = call(
        functools.partial(dispatch_kernel, capacity, share),
        [shape(2 * capacity, share)] * 3 + [shape(experts * capacity, count)],
        (ids, prob, tokens, grad_out),
        SMALL,
        8,
        [pltpu.VMEM((1, count), jnp.int32), pltpu.VMEM((1, count), F32)]
        + [pltpu.VMEM((count, share), BF16)] * 2
        + [pltpu.SemaphoreType.DMA((4,))],
        far=4,
    )
    got1 = swap(send1, "expert", 1)
    got3 = swap(send3, "expert", 3)
    total_rows = experts * capacity
    chunk_a = slice(0, 2 * capacity)
    chunk_own = slice(2 * capacity, 3 * capacity)
    chunk_b = slice(3 * capacity, 4 * capacity)
    shared = [shape(total_rows, width)] * 2 + [shape(total_rows, hidden_part)] * 3
    terms_a = [shape(4, 3 * capacity, share)] * 2
    terms_b = [shape(4, capacity, share)] * 2
    own_out = call(
        functools.partial(own_kernel, share, chunk_own),
        shared + terms_a + [shape(*w.shape) for w in weights],
        (prob, tokens, grad_out) + weights + (assign,),
        SMALL,
        20,
        [pltpu.VMEM((1, count), F32)]
        + [pltpu.VMEM((count, width), BF16)] * 2
        + [pltpu.SemaphoreType.DMA((6,))],
        far=6,
    )
    send2, *own_out = fence(send2, *own_out)
    block_b = swap(send2, "expert", 2)
    got1, got3, *own_out = fence(got1, got3, *own_out)
    weights = tuple(own_out[7:])

    block_a = jnp.concatenate(
        [got1[:capacity], got3[:capacity], got1[capacity:], got3[capacity:]], axis=0
    )
    first_a = swap_first(block_a)
    second_a = swap_second(block_a)
    first_a, block_b = fence(first_a, block_b)
    third_a = swap_second(first_a)
    first_b = swap_first(block_b)
    second_a, third_a, first_b = fence(second_a, third_a, first_b)

    across_a = swap(jnp.concatenate([block_a, first_a, second_a, third_a]), "dp", 1)
    pair_b = jnp.concatenate([block_b, first_b])
    both_b = swap_second(pair_b)
    early_b = swap(pair_b, "dp", 1)
    out_a = call(
        functools.partial(chunk_kernel, share, chunk_a, chunk_a, 1, 7),
        shared + terms_a,
        (block_a, first_a, second_a, third_a, across_a) + weights + tuple(own_out[:7]),
        SMALL,
        16,
        aliases={8 + j: j for j in range(7)},
    )
    both_b, early_b, *out_a = fence(both_b, early_b, *out_a)

    partial = call(
        functools.partial(early_kernel, share),
        [shape(capacity, hidden_part, dtype=F32)] * 3,
        (pair_b, both_b, early_b) + weights,
        SMALL,
        16,
    )
    later_b = swap(both_b, "dp", 1)
    later_b, *out_a = fence(later_b, *out_a, *partial)
    out_a, partial = out_a[:7], tuple(out_a[7:])
    other_a = swap(out_a[6], "dp", 1)
    out_b = call(
        functools.partial(late_kernel, share, chunk_b),
        shared + terms_b[:1],
        (pair_b, both_b, early_b, later_b)
        + partial
        + weights
        + tuple(out_a[:5]),
        SMALL,
        16,
        aliases={10 + j: j for j in range(5)},
    )
    other_a, *out_b = fence(other_a, *out_b)
    x_all, y_all, hidden, gate_grad, up_grad, odd_b = out_b
    (even_b,) = call(
        functools.partial(even_kernel, share, chunk_b),
        terms_b[:1],
        (gate_grad, up_grad) + weights[:2],
        SMALL,
        16,
    )
    other_b, even_b = fence(swap(odd_b, "dp", 1), even_b)

    def wgrad(left, right):
        blocks = 4
        scratch = [
            pltpu.VMEM((blocks, left.shape[1] // blocks, right.shape[1]), BF16),
            pltpu.SemaphoreType.DMA((blocks,)),
        ]
        (out,) = call(
            wgrad_kernel,
            [shape(left.shape[1], right.shape[1])],
            (left, right),
            SMALL,
            16,
            scratch,
            out_space=HBM,
        )
        return out

    pairs_a = core_pairs(out_a[5], other_a)
    pairs_b = core_pairs(even_b, other_b)
    pairs = [jnp.concatenate([pairs_a[j], pairs_b[j]]) for j in range(4)]
    relay = swap_second(pairs[3])
    late = swap_second(pairs[2])
    (relay,) = fence(relay)
    half = 2 * capacity
    step = total_of([pairs[1], relay])
    last_a = swap_first(step[:half])
    last_b = swap_first(step[half:])
    up_wgrad = wgrad(x_all, up_grad)
    last_a, late, up_wgrad, x_all = fence(last_a, late, up_wgrad, x_all)
    summed_a = total_of([pairs[0][:half], last_a, late[:half]])
    ret3 = swap(summed_a[capacity:], "expert", 3)
    ret1 = swap(summed_a[:capacity], "expert", 1)
    summed_a, last_b = fence(summed_a, last_b)
    summed_b = total_of([pairs[0][half:], last_b, late[half:]])
    ret0 = summed_b[:capacity]
    ret2 = swap(summed_b[capacity:], "expert", 2)
    gate_wgrad = wgrad(x_all, gate_grad)
    ret1, ret2, ret3, gate_wgrad = fence(ret1, ret2, ret3, gate_wgrad)
    (token_cols,) = call(
        combine_kernel,
        [shape(count, share)],
        (assign, ret0, ret1, ret2, ret3),
        SMALL,
        8,
        [pltpu.VMEM((experts * capacity, share), BF16)],
    )
    sixth = swap(token_cols, "dp", 6)
    first = swap_first(token_cols)
    second = swap_second(token_cols)
    down_wgrad = wgrad(hidden, y_all)
    first, second, sixth, down_wgrad = fence(first, second, sixth, down_wgrad)
    across = swap(jnp.concatenate([token_cols, first, second, sixth]), "dp", 1)
    (placed,) = call(
        functools.partial(place_kernel, share, 0, 4),
        [shape(count, width)],
        (token_cols, first, second, sixth),
        SMALL,
        8,
        [pltpu.SemaphoreType.DMA((4,))],
        out_space=HBM,
    )
    across, placed = fence(across, placed)
    (grad_tokens,) = pl.pallas_call(
        functools.partial(place_kernel, share, 1, 1),
        out_shape=[shape(count, width)],
        in_specs=[pl.BlockSpec(memory_space=VMEM), pl.BlockSpec(memory_space=HBM)],
        out_specs=[pl.BlockSpec(memory_space=HBM)],
        scratch_shapes=[pltpu.SemaphoreType.DMA((4,))],
        input_output_aliases={1: 0},
        compiler_params=pltpu.CompilerParams(vmem_limit_bytes=8 << 20),
    )(across, pltpu.with_memory_space_constraint(placed, HBM))
    return (grad_tokens, gate_wgrad[None], up_wgrad[None], down_wgrad[None])


def solution(mesh):
    placed = (
        P("expert", None),
        P("expert", None),
        P("expert", None),
        P("expert", None),
        P("expert", None, "dp"),
        P("expert", None, "dp"),
        P("expert", "dp", None),
    )
    fits = mesh.shape["dp"] == 8 and mesh.shape["expert"] == 4
    return jax.shard_map(
        per_device_blocks if fits else per_device_any,
        mesh=mesh,
        in_specs=placed,
        out_specs=(
            P("expert", None),
            P("expert", None, "dp"),
            P("expert", None, "dp"),
            P("expert", "dp", None),
        ),
        check_vma=False,
    )
```

```python
import functools
import jax
import jax.numpy as jnp
from jax import lax
from jax.experimental import pallas as pl
from jax.experimental.pallas import tpu as pltpu
from jax.sharding import PartitionSpec as P

BF16 = jnp.bfloat16
F32 = jnp.float32
LAST = (((1,), (1,)), ((), ()))
FIRST = (((0,), (0,)), ((), ()))
VMEM = pltpu.MemorySpace.VMEM


def silu_parts(pre_gate):
    sigma = jax.nn.sigmoid(pre_gate)
    return (pre_gate * sigma, sigma * (1.0 + pre_gate * (1.0 - sigma)))


def per_device_any(tokens, grad_out, expert_ids, gate_prob, w_gate, w_up, w_down):
    expert_count = lax.axis_size("expert")
    replica_count = lax.axis_size("dp")
    tok_count = tokens.shape[0]
    width_all = tokens.shape[1]
    capacity = max(2, (5 * tok_count + 2 * expert_count - 1) // (2 * expert_count))
    routed = expert_ids[:, 0]
    one_hot = (routed[:, None] == jnp.arange(expert_count, dtype=jnp.int32)[None, :]).astype(
        jnp.int32
    )
    slot_index = jnp.sum((jnp.cumsum(one_hot, axis=0) - one_hot) * one_hot, axis=1)
    target = routed * capacity + slot_index
    assign = (
        target[None, :] == jnp.arange(expert_count * capacity, dtype=jnp.int32)[:, None]
    ).astype(jnp.bfloat16)
    scaled = (gate_prob * grad_out.astype(jnp.float32)).astype(jnp.bfloat16)
    input_slots = jnp.dot(assign, tokens, preferred_element_type=jnp.float32).astype(jnp.bfloat16)
    scaled_slots = jnp.dot(assign, scaled, preferred_element_type=jnp.float32).astype(jnp.bfloat16)
    hidden_part = w_gate.shape[2]
    w_pair = jnp.concatenate([w_gate[0], w_up[0]], axis=1)
    down_rows = w_down[0]
    contract_last = (((1,), (1,)), ((), ()))
    contract_first = (((0,), (0,)), ((), ()))
    share = width_all // replica_count
    offset = lax.axis_index("dp") * share
    input_cols = lax.dynamic_slice_in_dim(input_slots, offset, share, 1)
    scaled_cols = lax.dynamic_slice_in_dim(scaled_slots, offset, share, 1)
    got_input, got_scaled = (
        lax.all_to_all(input_cols, "expert", split_axis=0, concat_axis=0, tiled=True),
        lax.all_to_all(scaled_cols, "expert", split_axis=0, concat_axis=0, tiled=True),
    )
    all_inputs, all_scaled = (
        lax.all_gather(got_input, "dp", axis=1, tiled=True),
        lax.all_gather(got_scaled, "dp", axis=1, tiled=True),
    )
    pre_act = jnp.dot(all_inputs, w_pair, preferred_element_type=jnp.float32)
    pre_gate = pre_act[:, :hidden_part]
    pre_up = pre_act[:, hidden_part:]
    activated, slope = silu_parts(pre_gate)
    hidden = (activated * pre_up).astype(jnp.bfloat16)
    hidden_grad = lax.dot_general(
        all_scaled, down_rows, contract_last, preferred_element_type=jnp.float32
    )
    down_grad = lax.dot_general(
        hidden, all_scaled, contract_first, preferred_element_type=jnp.float32
    )
    up_grad = (hidden_grad * activated).astype(jnp.bfloat16)
    gate_grad = (hidden_grad * pre_up * slope).astype(jnp.bfloat16)
    pair_grad = jnp.concatenate([gate_grad, up_grad], axis=1)
    weight_grad = lax.dot_general(
        all_inputs, pair_grad, contract_first, preferred_element_type=jnp.float32
    )
    terms = lax.dot_general(pair_grad, w_pair, contract_last, preferred_element_type=jnp.float32)
    weight_grad, down_grad, terms = (weight_grad, down_grad, terms)
    summed = lax.psum_scatter(terms.astype(jnp.bfloat16), "dp", scatter_dimension=1, tiled=True)
    returned_rows = lax.all_to_all(summed, "expert", split_axis=0, concat_axis=0, tiled=True)
    token_cols = lax.dot_general(
        assign, returned_rows, contract_first, preferred_element_type=jnp.float32
    ).astype(jnp.bfloat16)
    grad_tokens = lax.all_gather(token_cols, "dp", axis=1, tiled=True)
    gate_wgrad = weight_grad[:, :hidden_part].astype(jnp.bfloat16)
    up_wgrad = weight_grad[:, hidden_part:].astype(jnp.bfloat16)
    return (grad_tokens, gate_wgrad[None], up_wgrad[None], down_grad.astype(jnp.bfloat16)[None])


SMALL = 1000
HBM = pltpu.MemorySpace.HBM


def call(body, outs, operands, flops, limit, scratch=(), far=0, aliases=None, out_space=VMEM):
    nbytes = sum(a.size * a.dtype.itemsize for a in operands)
    nbytes += sum(o.size * o.dtype.itemsize for o in outs)
    return pl.pallas_call(
        body,
        out_shape=outs,
        in_specs=[pl.BlockSpec(memory_space=HBM)] * far
        + [pl.BlockSpec(memory_space=VMEM)] * (len(operands) - far),
        out_specs=[pl.BlockSpec(memory_space=out_space)] * len(outs),
        scratch_shapes=list(scratch),
        input_output_aliases=aliases or {},
        compiler_params=pltpu.CompilerParams(vmem_limit_bytes=limit << 20),
        cost_estimate=pl.CostEstimate(flops=flops, bytes_accessed=nbytes, transcendentals=0),
    )(*[pltpu.with_memory_space_constraint(a, HBM) for a in operands[:far]], *operands[far:])


def shape(*dims, dtype=BF16):
    return jax.ShapeDtypeStruct(dims, dtype)


def cols(block, width):
    return pl.ds(pl.multiple_of(block * width, width), width)


def column(row):
    return jnp.transpose(jnp.broadcast_to(row, (128, row.shape[1])))[:, 0:1]


def start_copies(sems, *pairs):
    copies = [pltpu.make_async_copy(src, dst, sems.at[j]) for j, (src, dst) in enumerate(pairs)]
    for copy in copies:
        copy.start()
    return copies


def dispatch_kernel(
    capacity, share, ids_far, prob_far, tok, grad, send1, send2, send3, assign,
    ids, prob, tok_part, grad_part, sems,
):
    here = lax.axis_index("expert")
    piece = cols(lax.axis_index("dp"), share)
    ids_copy, prob_copy, tok_copy, grad_copy = start_copies(
        sems,
        (ids_far, ids),
        (prob_far, prob),
        (tok.at[:, piece], tok_part),
        (grad.at[:, piece], grad_part),
    )
    count = tok.shape[0]
    places = assign.shape[0]
    row = lax.broadcasted_iota(jnp.int32, (count, count), 0)
    col = lax.broadcasted_iota(jnp.int32, (count, count), 1)
    earlier = (row < col).astype(F32).astype(BF16)
    expert = lax.broadcasted_iota(jnp.int32, (8, count), 0)
    spots = lax.broadcasted_iota(jnp.int32, (places, count), 0)
    ids_copy.wait()
    relative = jnp.bitwise_xor(ids[...], here)
    hit = (relative == expert).astype(F32)
    before = jnp.dot(hit.astype(BF16), earlier, preferred_element_type=F32)
    slot = jnp.sum(before * hit, axis=0, keepdims=True).astype(jnp.int32)
    target = relative * capacity + slot
    chosen = (target == spots).astype(F32).astype(BF16)
    assign[...] = chosen
    prob_copy.wait()
    weight = column(prob[...])
    tok_copy.wait()
    grad_copy.wait()
    y_part = (weight * grad_part[...].astype(F32)).astype(BF16)
    both = jnp.concatenate([tok_part[...], y_part], axis=1)
    for k, ref in ((1, send1), (3, send3), (2, send2)):
        pick = chosen[k * capacity : (k + 1) * capacity]
        rows = jnp.dot(pick, both, preferred_element_type=F32).astype(BF16)
        ref[:capacity] = rows[:, :share]
        ref[capacity:] = rows[:, share:]


def block_order():
    core = jnp.bitwise_and(lax.axis_index("dp"), 1)
    first = 2 + 2 * core
    second = 4 - 2 * core
    return (0, first, second, 6), (1, second + 1, first + 1, 7)


def forward_sums(parts, weights, ready=(lambda: None,) * 3):
    sums = []
    for weight, wait in zip(weights, ready):
        wait()
        total = 0.0
        for x_part, y_part, piece in parts:
            if weight is weights[2]:
                total += lax.dot_general(
                    y_part, weight[:, piece], LAST, preferred_element_type=F32
                )
            else:
                total += jnp.dot(x_part, weight[piece, :], preferred_element_type=F32)
        sums.append(total)
    return sums


def gradients(sums, hidden, gate_grad, up_grad, rows):
    pre_gate, pre_up, hidden_grad = sums
    activated, slope = silu_parts(pre_gate)
    hidden[rows] = (activated * pre_up).astype(BF16)
    gate_grad[rows] = (hidden_grad * pre_up * slope).astype(BF16)
    up_grad[rows] = (hidden_grad * activated).astype(BF16)


def input_terms(share, order, gate_part, up_part, w_gate, w_up, out, spot):
    block = lax.axis_index("dp")
    for j, k in enumerate(order):
        piece = cols(jnp.bitwise_xor(block, k), share)
        term = lax.dot_general(gate_part, w_gate[piece, :], LAST, preferred_element_type=F32)
        term += lax.dot_general(up_part, w_up[piece, :], LAST, preferred_element_type=F32)
        out[j, spot] = term.astype(BF16)


def expert_math(share, rows, spot, shared, terms, weights, ready=(lambda: None,) * 3):
    x_all, y_all, hidden, gate_grad, up_grad = shared
    sums = forward_sums([(x_all[rows], y_all[rows], slice(None))], weights, ready)
    gradients(sums, hidden, gate_grad, up_grad, rows)
    mine, across = block_order()
    for out, order in zip(terms, (mine, across)):
        input_terms(share, order, gate_grad[rows], up_grad[rows], weights[0], weights[1], out, spot)


def early_kernel(share, *refs):
    blocks = parts_of(refs[0], 2) + parts_of(refs[1], 2) + parts_of(refs[2], 2)
    weights, outs = refs[3:6], refs[6:]
    block = lax.axis_index("dp")
    mine, across = block_order()
    parts = []
    for k, ref in zip(mine + across[:2], blocks):
        x_part, y_part = halves_of(ref)
        parts.append((x_part[...], y_part[...], cols(jnp.bitwise_xor(block, k), share)))
    for out, total in zip(outs, forward_sums(parts, weights)):
        out[...] = total


def late_kernel(share, rows, *refs):
    blocks = [part for ref in refs[:4] for part in parts_of(ref, 2)]
    early, weights = refs[4:7], refs[7:10]
    x_all, y_all, hidden, gate_grad, up_grad, odd = refs[15:]
    block = lax.axis_index("dp")
    mine, across = block_order()
    parts = []
    for k, ref in zip(mine + across, blocks):
        x_part, y_part = halves_of(ref)
        piece = cols(jnp.bitwise_xor(block, k), share)
        x_all[rows, piece] = x_part[...]
        y_all[rows, piece] = y_part[...]
        parts.append((x_part, y_part, piece))
    parts = [(x_part[...], y_part[...], piece) for x_part, y_part, piece in parts[6:]]
    sums = [total + part[...] for total, part in zip(forward_sums(parts, weights), early)]
    gradients(sums, hidden, gate_grad, up_grad, rows)
    input_terms(
        share, across, gate_grad[rows], up_grad[rows], weights[0], weights[1], odd, slice(None)
    )


def even_kernel(share, rows, gate_grad, up_grad, w_gate, w_up, even):
    mine, _ = block_order()
    input_terms(share, mine, gate_grad[rows], up_grad[rows], w_gate, w_up, even, slice(None))


def own_kernel(
    share, spot, prob_far, tok_far, grad_far, gate_far, up_far, down_far, assign,
    x_all, y_all, hidden, gate_grad, up_grad, even, odd, w_gate, w_up, w_down,
    prob, tok, grad, sems,
):
    prob_copy, tok_copy, grad_copy, *weight_copies = start_copies(
        sems,
        (prob_far, prob),
        (tok_far, tok),
        (grad_far, grad),
        (gate_far, w_gate),
        (up_far, w_up),
        (down_far, w_down),
    )
    own = assign[: spot.stop - spot.start]
    tok_copy.wait()
    x_all[spot] = jnp.dot(own, tok[...], preferred_element_type=F32).astype(BF16)
    prob_copy.wait()
    grad_copy.wait()
    scaled = (column(prob[...]) * grad[...].astype(F32)).astype(BF16)
    y_all[spot] = jnp.dot(own, scaled, preferred_element_type=F32).astype(BF16)
    expert_math(
        share, spot, spot, (x_all, y_all, hidden, gate_grad, up_grad), (even, odd),
        (w_gate, w_up, w_down), [copy.wait for copy in weight_copies],
    )


def chunk_kernel(share, rows, spot, pieces, extra, *refs):
    blocks = list(refs[:4])
    for ref in refs[4 : 4 + pieces]:
        blocks += parts_of(ref, 4 // pieces)
    rest = refs[4 + pieces :]
    weights = rest[:3]
    outs = rest[3 + extra :]
    x_all, y_all = outs[:2]
    block = lax.axis_index("dp")
    mine, across = block_order()
    for k, ref in zip(mine + across, blocks):
        x_part, y_part = halves_of(ref)
        piece = cols(jnp.bitwise_xor(block, k), share)
        x_all[rows, piece] = x_part[...]
        y_all[rows, piece] = y_part[...]
    expert_math(share, rows, spot, outs[:5], outs[5:7], weights)


def wgrad_kernel(left, right, out, tile, sems):
    blocks = tile.shape[0]
    rows = tile.shape[1]
    copies = []
    for j in range(blocks):
        part = left[:, j * rows : (j + 1) * rows]
        total = lax.dot_general(part, right[...], FIRST, preferred_element_type=F32)
        tile[j] = total.astype(BF16)
        copy = pltpu.make_async_copy(tile.at[j], out.at[pl.ds(j * rows, rows)], sems.at[j])
        copy.start()
        copies.append(copy)
    for copy in copies:
        copy.wait()


def combine_kernel(assign, r0, r1, r2, r3, out, rows):
    capacity = r0.shape[0]
    for k, ref in enumerate((r0, r1, r2, r3)):
        rows[k * capacity : (k + 1) * capacity] = ref[...]
    out[...] = lax.dot_general(assign[...], rows[...], FIRST, preferred_element_type=F32).astype(BF16)


def place_kernel(share, side, count, *refs):
    out, sems = refs[-2:]
    block = lax.axis_index("dp")
    pieces = [cols(jnp.bitwise_xor(block, k), share) for k in block_order()[side]]
    blocks = refs[:4] if count == 4 else parts_of(refs[0], 4)
    for copy in start_copies(sems, *[(b, out.at[:, p]) for b, p in zip(blocks, pieces)]):
        copy.wait()


def fence(*arrays):
    return lax.optimization_barrier(arrays)


def swap(array, axis, distance):
    size = lax.axis_size(axis)
    return lax.ppermute(array, axis, [(i, i ^ distance) for i in range(size)])


def halves_of(ref):
    half = ref.shape[0] // 2
    return (ref.at[pl.ds(0, half)], ref.at[pl.ds(half, half)])


def parts_of(ref, count):
    rows = ref.shape[0] // count
    return [ref.at[pl.ds(j * rows, rows)] for j in range(count)]


def swap_first(array):
    return lax.ppermute(array, "dp", [(i, i ^ (4 if i % 2 else 2)) for i in range(8)])


def swap_second(array):
    return lax.ppermute(array, "dp", [(i, i ^ (2 if i % 2 else 4)) for i in range(8)])


def core_pairs(even, other):
    return [(even[j].astype(F32) + other[j].astype(F32)).astype(BF16) for j in range(4)]


def total_of(parts):
    return sum(part.astype(F32) for part in parts).astype(BF16)


def per_device_blocks(tokens, grad_out, expert_ids, gate_prob, w_gate, w_up, w_down):
    count, width = tokens.shape
    experts = lax.axis_size("expert")
    share = width // lax.axis_size("dp")
    capacity = max(2, (5 * count + 2 * experts - 1) // (2 * experts))
    hidden_part = w_gate.shape[2]
    weights = (w_gate[0], w_up[0], w_down[0])

    ids = expert_ids.T
    prob = gate_prob.T
    send1, send2, send3, assign = call(
        functools.partial(dispatch_kernel, capacity, share),
        [shape(2 * capacity, share)] * 3 + [shape(experts * capacity, count)],
        (ids, prob, tokens, grad_out),
        SMALL,
        8,
        [pltpu.VMEM((1, count), jnp.int32), pltpu.VMEM((1, count), F32)]
        + [pltpu.VMEM((count, share), BF16)] * 2
        + [pltpu.SemaphoreType.DMA((4,))],
        far=4,
    )
    got1 = swap(send1, "expert", 1)
    got3 = swap(send3, "expert", 3)
    total_rows = experts * capacity
    chunk_a = slice(0, 2 * capacity)
    chunk_own = slice(2 * capacity, 3 * capacity)
    chunk_b = slice(3 * capacity, 4 * capacity)
    shared = [shape(total_rows, width)] * 2 + [shape(total_rows, hidden_part)] * 3
    terms_a = [shape(4, 3 * capacity, share)] * 2
    terms_b = [shape(4, capacity, share)] * 2
    own_out = call(
        functools.partial(own_kernel, share, chunk_own),
        shared + terms_a + [shape(*w.shape) for w in weights],
        (prob, tokens, grad_out) + weights + (assign,),
        SMALL,
        20,
        [pltpu.VMEM((1, count), F32)]
        + [pltpu.VMEM((count, width), BF16)] * 2
        + [pltpu.SemaphoreType.DMA((6,))],
        far=6,
    )
    send2, *own_out = fence(send2, *own_out)
    block_b = swap(send2, "expert", 2)
    got1, got3, *own_out = fence(got1, got3, *own_out)
    weights = tuple(own_out[7:])

    block_a = jnp.concatenate(
        [got1[:capacity], got3[:capacity], got1[capacity:], got3[capacity:]], axis=0
    )
    first_a = swap_first(block_a)
    second_a = swap_second(block_a)
    first_a, block_b = fence(first_a, block_b)
    third_a = swap_second(first_a)
    first_b = swap_first(block_b)
    second_a, third_a, first_b = fence(second_a, third_a, first_b)

    across_a = swap(jnp.concatenate([block_a, first_a, second_a, third_a]), "dp", 1)
    pair_b = jnp.concatenate([block_b, first_b])
    both_b = swap_second(pair_b)
    early_b = swap(pair_b, "dp", 1)
    out_a = call(
        functools.partial(chunk_kernel, share, chunk_a, chunk_a, 1, 7),
        shared + terms_a,
        (block_a, first_a, second_a, third_a, across_a) + weights + tuple(own_out[:7]),
        SMALL,
        16,
        aliases={8 + j: j for j in range(7)},
    )
    both_b, early_b, *out_a = fence(both_b, early_b, *out_a)

    partial = call(
        functools.partial(early_kernel, share),
        [shape(capacity, hidden_part, dtype=F32)] * 3,
        (pair_b, both_b, early_b) + weights,
        SMALL,
        16,
    )
    later_b = swap(both_b, "dp", 1)
    later_b, *out_a = fence(later_b, *out_a, *partial)
    out_a, partial = out_a[:7], tuple(out_a[7:])
    other_a = swap(out_a[6], "dp", 1)
    out_b = call(
        functools.partial(late_kernel, share, chunk_b),
        shared + terms_b[:1],
        (pair_b, both_b, early_b, later_b)
        + partial
        + weights
        + tuple(out_a[:5]),
        SMALL,
        16,
        aliases={10 + j: j for j in range(5)},
    )
    other_a, *out_b = fence(other_a, *out_b)
    x_all, y_all, hidden, gate_grad, up_grad, odd_b = out_b
    (even_b,) = call(
        functools.partial(even_kernel, share, chunk_b),
        terms_b[:1],
        (gate_grad, up_grad) + weights[:2],
        SMALL,
        16,
    )
    other_b, even_b = fence(swap(odd_b, "dp", 1), even_b)

    def wgrad(left, right):
        blocks = 4
        scratch = [
            pltpu.VMEM((blocks, left.shape[1] // blocks, right.shape[1]), BF16),
            pltpu.SemaphoreType.DMA((blocks,)),
        ]
        (out,) = call(
            wgrad_kernel,
            [shape(left.shape[1], right.shape[1])],
            (left, right),
            SMALL,
            16,
            scratch,
            out_space=HBM,
        )
        return out

    pairs_a = core_pairs(out_a[5], other_a)
    pairs_b = core_pairs(even_b, other_b)
    pairs = [jnp.concatenate([pairs_a[j], pairs_b[j]]) for j in range(4)]
    relay = swap_second(pairs[3])
    late = swap_second(pairs[2])
    (relay,) = fence(relay)
    half = 2 * capacity
    step = total_of([pairs[1], relay])
    last_a = swap_first(step[:half])
    last_b = swap_first(step[half:])
    up_wgrad = wgrad(x_all, up_grad)
    last_a, late, up_wgrad, x_all = fence(last_a, late, up_wgrad, x_all)
    summed_a = total_of([pairs[0][:half], last_a, late[:half]])
    ret3 = swap(summed_a[capacity:], "expert", 3)
    ret1 = swap(summed_a[:capacity], "expert", 1)
    summed_a, last_b = fence(summed_a, last_b)
    summed_b = total_of([pairs[0][half:], last_b, late[half:]])
    ret0 = summed_b[:capacity]
    ret2 = swap(summed_b[capacity:], "expert", 2)
    gate_wgrad = wgrad(x_all, gate_grad)
    ret1, ret2, ret3, gate_wgrad = fence(ret1, ret2, ret3, gate_wgrad)
    (token_cols,) = call(
        combine_kernel,
        [shape(count, share)],
        (assign, ret0, ret1, ret2, ret3),
        SMALL,
        8,
        [pltpu.VMEM((experts * capacity, share), BF16)],
    )
    sixth = swap(token_cols, "dp", 6)
    first = swap_first(token_cols)
    second = swap_second(token_cols)
    down_wgrad = wgrad(hidden, y_all)
    sixth, first, second, down_wgrad = fence(sixth, first, second, down_wgrad)
    across = swap(jnp.concatenate([token_cols, first, second, sixth]), "dp", 1)
    (placed,) = call(
        functools.partial(place_kernel, share, 0, 4),
        [shape(count, width)],
        (token_cols, first, second, sixth),
        SMALL,
        8,
        [pltpu.SemaphoreType.DMA((4,))],
        out_space=HBM,
    )
    across, placed = fence(across, placed)
    (grad_tokens,) = pl.pallas_call(
        functools.partial(place_kernel, share, 1, 1),
        out_shape=[shape(count, width)],
        in_specs=[pl.BlockSpec(memory_space=VMEM), pl.BlockSpec(memory_space=HBM)],
        out_specs=[pl.BlockSpec(memory_space=HBM)],
        scratch_shapes=[pltpu.SemaphoreType.DMA((4,))],
        input_output_aliases={1: 0},
        compiler_params=pltpu.CompilerParams(vmem_limit_bytes=8 << 20),
    )(across, pltpu.with_memory_space_constraint(placed, HBM))
    return (grad_tokens, gate_wgrad[None], up_wgrad[None], down_wgrad[None])


def solution(mesh):
    placed = (
        P("expert", None),
        P("expert", None),
        P("expert", None),
        P("expert", None),
        P("expert", None, "dp"),
        P("expert", None, "dp"),
        P("expert", "dp", None),
    )
    fits = mesh.shape["dp"] == 8 and mesh.shape["expert"] == 4
    return jax.shard_map(
        per_device_blocks if fits else per_device_any,
        mesh=mesh,
        in_specs=placed,
        out_specs=(
            P("expert", None),
            P("expert", None, "dp"),
            P("expert", None, "dp"),
            P("expert", "dp", None),
        ),
        check_vma=False,
    )
```

```python
import functools
import jax
import jax.numpy as jnp
from jax import lax
from jax.experimental import pallas as pl
from jax.experimental.pallas import tpu as pltpu
from jax.sharding import PartitionSpec as P

BF16 = jnp.bfloat16
F32 = jnp.float32
LAST = (((1,), (1,)), ((), ()))
FIRST = (((0,), (0,)), ((), ()))
VMEM = pltpu.MemorySpace.VMEM


def silu_parts(pre_gate):
    sigma = jax.nn.sigmoid(pre_gate)
    return (pre_gate * sigma, sigma * (1.0 + pre_gate * (1.0 - sigma)))


def per_device_any(tokens, grad_out, expert_ids, gate_prob, w_gate, w_up, w_down):
    expert_count = lax.axis_size("expert")
    replica_count = lax.axis_size("dp")
    tok_count = tokens.shape[0]
    width_all = tokens.shape[1]
    capacity = max(2, (5 * tok_count + 2 * expert_count - 1) // (2 * expert_count))
    routed = expert_ids[:, 0]
    one_hot = (routed[:, None] == jnp.arange(expert_count, dtype=jnp.int32)[None, :]).astype(
        jnp.int32
    )
    slot_index = jnp.sum((jnp.cumsum(one_hot, axis=0) - one_hot) * one_hot, axis=1)
    target = routed * capacity + slot_index
    assign = (
        target[None, :] == jnp.arange(expert_count * capacity, dtype=jnp.int32)[:, None]
    ).astype(jnp.bfloat16)
    scaled = (gate_prob * grad_out.astype(jnp.float32)).astype(jnp.bfloat16)
    input_slots = jnp.dot(assign, tokens, preferred_element_type=jnp.float32).astype(jnp.bfloat16)
    scaled_slots = jnp.dot(assign, scaled, preferred_element_type=jnp.float32).astype(jnp.bfloat16)
    hidden_part = w_gate.shape[2]
    w_pair = jnp.concatenate([w_gate[0], w_up[0]], axis=1)
    down_rows = w_down[0]
    contract_last = (((1,), (1,)), ((), ()))
    contract_first = (((0,), (0,)), ((), ()))
    share = width_all // replica_count
    offset = lax.axis_index("dp") * share
    input_cols = lax.dynamic_slice_in_dim(input_slots, offset, share, 1)
    scaled_cols = lax.dynamic_slice_in_dim(scaled_slots, offset, share, 1)
    got_input, got_scaled = (
        lax.all_to_all(input_cols, "expert", split_axis=0, concat_axis=0, tiled=True),
        lax.all_to_all(scaled_cols, "expert", split_axis=0, concat_axis=0, tiled=True),
    )
    all_inputs, all_scaled = (
        lax.all_gather(got_input, "dp", axis=1, tiled=True),
        lax.all_gather(got_scaled, "dp", axis=1, tiled=True),
    )
    pre_act = jnp.dot(all_inputs, w_pair, preferred_element_type=jnp.float32)
    pre_gate = pre_act[:, :hidden_part]
    pre_up = pre_act[:, hidden_part:]
    activated, slope = silu_parts(pre_gate)
    hidden = (activated * pre_up).astype(jnp.bfloat16)
    hidden_grad = lax.dot_general(
        all_scaled, down_rows, contract_last, preferred_element_type=jnp.float32
    )
    down_grad = lax.dot_general(
        hidden, all_scaled, contract_first, preferred_element_type=jnp.float32
    )
    up_grad = (hidden_grad * activated).astype(jnp.bfloat16)
    gate_grad = (hidden_grad * pre_up * slope).astype(jnp.bfloat16)
    pair_grad = jnp.concatenate([gate_grad, up_grad], axis=1)
    weight_grad = lax.dot_general(
        all_inputs, pair_grad, contract_first, preferred_element_type=jnp.float32
    )
    terms = lax.dot_general(pair_grad, w_pair, contract_last, preferred_element_type=jnp.float32)
    weight_grad, down_grad, terms = (weight_grad, down_grad, terms)
    summed = lax.psum_scatter(terms.astype(jnp.bfloat16), "dp", scatter_dimension=1, tiled=True)
    returned_rows = lax.all_to_all(summed, "expert", split_axis=0, concat_axis=0, tiled=True)
    token_cols = lax.dot_general(
        assign, returned_rows, contract_first, preferred_element_type=jnp.float32
    ).astype(jnp.bfloat16)
    grad_tokens = lax.all_gather(token_cols, "dp", axis=1, tiled=True)
    gate_wgrad = weight_grad[:, :hidden_part].astype(jnp.bfloat16)
    up_wgrad = weight_grad[:, hidden_part:].astype(jnp.bfloat16)
    return (grad_tokens, gate_wgrad[None], up_wgrad[None], down_grad.astype(jnp.bfloat16)[None])


SMALL = 1000
HBM = pltpu.MemorySpace.HBM


def call(body, outs, operands, flops, limit, scratch=(), far=0, aliases=None, out_space=VMEM):
    nbytes = sum(a.size * a.dtype.itemsize for a in operands)
    nbytes += sum(o.size * o.dtype.itemsize for o in outs)
    return pl.pallas_call(
        body,
        out_shape=outs,
        in_specs=[pl.BlockSpec(memory_space=HBM)] * far
        + [pl.BlockSpec(memory_space=VMEM)] * (len(operands) - far),
        out_specs=[pl.BlockSpec(memory_space=out_space)] * len(outs),
        scratch_shapes=list(scratch),
        input_output_aliases=aliases or {},
        compiler_params=pltpu.CompilerParams(vmem_limit_bytes=limit << 20),
        cost_estimate=pl.CostEstimate(flops=flops, bytes_accessed=nbytes, transcendentals=0),
    )(*[pltpu.with_memory_space_constraint(a, HBM) for a in operands[:far]], *operands[far:])


def shape(*dims, dtype=BF16):
    return jax.ShapeDtypeStruct(dims, dtype)


def cols(block, width):
    return pl.ds(pl.multiple_of(block * width, width), width)


def column(row):
    return jnp.transpose(jnp.broadcast_to(row, (128, row.shape[1])))[:, 0:1]


def start_copies(sems, *pairs):
    copies = [pltpu.make_async_copy(src, dst, sems.at[j]) for j, (src, dst) in enumerate(pairs)]
    for copy in copies:
        copy.start()
    return copies


def dispatch_kernel(
    capacity, share, ids_far, prob_far, tok, grad, send1, send2, send3, assign,
    ids, prob, tok_part, grad_part, sems,
):
    here = lax.axis_index("expert")
    piece = cols(lax.axis_index("dp"), share)
    ids_copy, prob_copy, tok_copy, grad_copy = start_copies(
        sems,
        (ids_far, ids),
        (prob_far, prob),
        (tok.at[:, piece], tok_part),
        (grad.at[:, piece], grad_part),
    )
    count = tok.shape[0]
    places = assign.shape[0]
    row = lax.broadcasted_iota(jnp.int32, (count, count), 0)
    col = lax.broadcasted_iota(jnp.int32, (count, count), 1)
    earlier = (row < col).astype(F32).astype(BF16)
    expert = lax.broadcasted_iota(jnp.int32, (8, count), 0)
    spots = lax.broadcasted_iota(jnp.int32, (places, count), 0)
    ids_copy.wait()
    relative = jnp.bitwise_xor(ids[...], here)
    hit = (relative == expert).astype(F32)
    before = jnp.dot(hit.astype(BF16), earlier, preferred_element_type=F32)
    slot = jnp.sum(before * hit, axis=0, keepdims=True).astype(jnp.int32)
    target = relative * capacity + slot
    chosen = (target == spots).astype(F32).astype(BF16)
    assign[...] = chosen
    prob_copy.wait()
    weight = column(prob[...])
    tok_copy.wait()
    grad_copy.wait()
    y_part = (weight * grad_part[...].astype(F32)).astype(BF16)
    both = jnp.concatenate([tok_part[...], y_part], axis=1)
    for k, ref in ((1, send1), (3, send3), (2, send2)):
        pick = chosen[k * capacity : (k + 1) * capacity]
        rows = jnp.dot(pick, both, preferred_element_type=F32).astype(BF16)
        ref[:capacity] = rows[:, :share]
        ref[capacity:] = rows[:, share:]


def block_order():
    core = jnp.bitwise_and(lax.axis_index("dp"), 1)
    first = 2 + 2 * core
    second = 4 - 2 * core
    return (0, first, second, 6), (1, second + 1, first + 1, 7)


def forward_sums(parts, weights, ready=(lambda: None,) * 3):
    sums = []
    for weight, wait in zip(weights, ready):
        wait()
        total = 0.0
        for x_part, y_part, piece in parts:
            if weight is weights[2]:
                total += lax.dot_general(
                    y_part, weight[:, piece], LAST, preferred_element_type=F32
                )
            else:
                total += jnp.dot(x_part, weight[piece, :], preferred_element_type=F32)
        sums.append(total)
    return sums


def gradients(sums, hidden, gate_grad, up_grad, rows):
    pre_gate, pre_up, hidden_grad = sums
    activated, slope = silu_parts(pre_gate)
    hidden[rows] = (activated * pre_up).astype(BF16)
    gate_grad[rows] = (hidden_grad * pre_up * slope).astype(BF16)
    up_grad[rows] = (hidden_grad * activated).astype(BF16)


def input_terms(share, order, gate_part, up_part, w_gate, w_up, out, spot):
    block = lax.axis_index("dp")
    for j, k in enumerate(order):
        piece = cols(jnp.bitwise_xor(block, k), share)
        term = lax.dot_general(gate_part, w_gate[piece, :], LAST, preferred_element_type=F32)
        term += lax.dot_general(up_part, w_up[piece, :], LAST, preferred_element_type=F32)
        out[j, spot] = term.astype(BF16)


def expert_math(share, rows, spot, shared, terms, weights, ready=(lambda: None,) * 3):
    x_all, y_all, hidden, gate_grad, up_grad = shared
    sums = forward_sums([(x_all[rows], y_all[rows], slice(None))], weights, ready)
    gradients(sums, hidden, gate_grad, up_grad, rows)
    mine, across = block_order()
    for out, order in zip(terms, (mine, across)):
        input_terms(share, order, gate_grad[rows], up_grad[rows], weights[0], weights[1], out, spot)


def early_kernel(share, *refs):
    blocks = parts_of(refs[0], 2) + parts_of(refs[1], 2) + parts_of(refs[2], 2)
    weights, outs = refs[3:6], refs[6:]
    block = lax.axis_index("dp")
    mine, across = block_order()
    parts = []
    for k, ref in zip(mine + across[:2], blocks):
        x_part, y_part = halves_of(ref)
        parts.append((x_part[...], y_part[...], cols(jnp.bitwise_xor(block, k), share)))
    for out, total in zip(outs, forward_sums(parts, weights)):
        out[...] = total


def late_kernel(share, rows, *refs):
    blocks = [part for ref in refs[:4] for part in parts_of(ref, 2)]
    early, weights = refs[4:7], refs[7:10]
    x_all, y_all, hidden, gate_grad, up_grad, odd = refs[15:]
    block = lax.axis_index("dp")
    mine, across = block_order()
    parts = []
    for k, ref in zip(mine + across, blocks):
        x_part, y_part = halves_of(ref)
        piece = cols(jnp.bitwise_xor(block, k), share)
        x_all[rows, piece] = x_part[...]
        y_all[rows, piece] = y_part[...]
        parts.append((x_part, y_part, piece))
    parts = [(x_part[...], y_part[...], piece) for x_part, y_part, piece in parts[6:]]
    sums = [total + part[...] for total, part in zip(forward_sums(parts, weights), early)]
    gradients(sums, hidden, gate_grad, up_grad, rows)
    input_terms(
        share, across, gate_grad[rows], up_grad[rows], weights[0], weights[1], odd, slice(None)
    )


def even_kernel(share, rows, gate_grad, up_grad, w_gate, w_up, even):
    mine, _ = block_order()
    input_terms(share, mine, gate_grad[rows], up_grad[rows], w_gate, w_up, even, slice(None))


def own_kernel(
    share, spot, prob_far, tok_far, grad_far, gate_far, up_far, down_far, assign,
    x_all, y_all, hidden, gate_grad, up_grad, even, odd, w_gate, w_up, w_down,
    prob, tok, grad, sems,
):
    prob_copy, tok_copy, grad_copy, *weight_copies = start_copies(
        sems,
        (prob_far, prob),
        (tok_far, tok),
        (grad_far, grad),
        (gate_far, w_gate),
        (up_far, w_up),
        (down_far, w_down),
    )
    own = assign[: spot.stop - spot.start]
    tok_copy.wait()
    x_all[spot] = jnp.dot(own, tok[...], preferred_element_type=F32).astype(BF16)
    prob_copy.wait()
    grad_copy.wait()
    scaled = (column(prob[...]) * grad[...].astype(F32)).astype(BF16)
    y_all[spot] = jnp.dot(own, scaled, preferred_element_type=F32).astype(BF16)
    expert_math(
        share, spot, spot, (x_all, y_all, hidden, gate_grad, up_grad), (even, odd),
        (w_gate, w_up, w_down), [copy.wait for copy in weight_copies],
    )


def chunk_kernel(share, rows, spot, pieces, extra, *refs):
    blocks = list(refs[:4])
    for ref in refs[4 : 4 + pieces]:
        blocks += parts_of(ref, 4 // pieces)
    rest = refs[4 + pieces :]
    weights = rest[:3]
    outs = rest[3 + extra :]
    x_all, y_all = outs[:2]
    block = lax.axis_index("dp")
    mine, across = block_order()
    for k, ref in zip(mine + across, blocks):
        x_part, y_part = halves_of(ref)
        piece = cols(jnp.bitwise_xor(block, k), share)
        x_all[rows, piece] = x_part[...]
        y_all[rows, piece] = y_part[...]
    expert_math(share, rows, spot, outs[:5], outs[5:7], weights)


def wgrad_kernel(left, right, out, tile, sems):
    blocks = tile.shape[0]
    rows = tile.shape[1]
    copies = []
    for j in range(blocks):
        part = left[:, j * rows : (j + 1) * rows]
        total = lax.dot_general(part, right[...], FIRST, preferred_element_type=F32)
        tile[j] = total.astype(BF16)
        copy = pltpu.make_async_copy(tile.at[j], out.at[pl.ds(j * rows, rows)], sems.at[j])
        copy.start()
        copies.append(copy)
    for copy in copies:
        copy.wait()


def combine_kernel(assign, r0, r1, r2, r3, out, rows):
    capacity = r0.shape[0]
    for k, ref in enumerate((r0, r1, r2, r3)):
        rows[k * capacity : (k + 1) * capacity] = ref[...]
    out[...] = lax.dot_general(assign[...], rows[...], FIRST, preferred_element_type=F32).astype(BF16)


def place_kernel(share, side, count, *refs):
    out, sems = refs[-2:]
    block = lax.axis_index("dp")
    pieces = [cols(jnp.bitwise_xor(block, k), share) for k in block_order()[side]]
    blocks = refs[:4] if count == 4 else parts_of(refs[0], 4)
    for copy in start_copies(sems, *[(b, out.at[:, p]) for b, p in zip(blocks, pieces)]):
        copy.wait()


def fence(*arrays):
    return lax.optimization_barrier(arrays)


def swap(array, axis, distance):
    size = lax.axis_size(axis)
    return lax.ppermute(array, axis, [(i, i ^ distance) for i in range(size)])


def halves_of(ref):
    half = ref.shape[0] // 2
    return (ref.at[pl.ds(0, half)], ref.at[pl.ds(half, half)])


def parts_of(ref, count):
    rows = ref.shape[0] // count
    return [ref.at[pl.ds(j * rows, rows)] for j in range(count)]


def swap_first(array):
    return lax.ppermute(array, "dp", [(i, i ^ (4 if i % 2 else 2)) for i in range(8)])


def swap_second(array):
    return lax.ppermute(array, "dp", [(i, i ^ (2 if i % 2 else 4)) for i in range(8)])


def core_pairs(even, other):
    return [(even[j].astype(F32) + other[j].astype(F32)).astype(BF16) for j in range(4)]


def total_of(parts):
    return sum(part.astype(F32) for part in parts).astype(BF16)


def per_device_blocks(tokens, grad_out, expert_ids, gate_prob, w_gate, w_up, w_down):
    count, width = tokens.shape
    experts = lax.axis_size("expert")
    share = width // lax.axis_size("dp")
    capacity = max(2, (5 * count + 2 * experts - 1) // (2 * experts))
    hidden_part = w_gate.shape[2]
    weights = (w_gate[0], w_up[0], w_down[0])

    ids = expert_ids.T
    prob = gate_prob.T
    send1, send2, send3, assign = call(
        functools.partial(dispatch_kernel, capacity, share),
        [shape(2 * capacity, share)] * 3 + [shape(experts * capacity, count)],
        (ids, prob, tokens, grad_out),
        SMALL,
        8,
        [pltpu.VMEM((1, count), jnp.int32), pltpu.VMEM((1, count), F32)]
        + [pltpu.VMEM((count, share), BF16)] * 2
        + [pltpu.SemaphoreType.DMA((4,))],
        far=4,
    )
    got1 = swap(send1, "expert", 1)
    got3 = swap(send3, "expert", 3)
    total_rows = experts * capacity
    chunk_a = slice(0, 2 * capacity)
    chunk_own = slice(2 * capacity, 3 * capacity)
    chunk_b = slice(3 * capacity, 4 * capacity)
    shared = [shape(total_rows, width)] * 2 + [shape(total_rows, hidden_part)] * 3
    terms_a = [shape(4, 3 * capacity, share)] * 2
    terms_b = [shape(4, capacity, share)] * 2
    own_out = call(
        functools.partial(own_kernel, share, chunk_own),
        shared + terms_a + [shape(*w.shape) for w in weights],
        (prob, tokens, grad_out) + weights + (assign,),
        SMALL,
        20,
        [pltpu.VMEM((1, count), F32)]
        + [pltpu.VMEM((count, width), BF16)] * 2
        + [pltpu.SemaphoreType.DMA((6,))],
        far=6,
    )
    send2, *own_out = fence(send2, *own_out)
    block_b = swap(send2, "expert", 2)
    got1, got3, *own_out = fence(got1, got3, *own_out)
    weights = tuple(own_out[7:])

    block_a = jnp.concatenate(
        [got1[:capacity], got3[:capacity], got1[capacity:], got3[capacity:]], axis=0
    )
    first_a = swap_first(block_a)
    second_a = swap_second(block_a)
    first_a, block_b = fence(first_a, block_b)
    third_a = swap_second(first_a)
    first_b = swap_first(block_b)
    second_a, third_a, first_b = fence(second_a, third_a, first_b)

    across_a = swap(jnp.concatenate([block_a, first_a, second_a, third_a]), "dp", 1)
    pair_b = jnp.concatenate([block_b, first_b])
    both_b = swap_second(pair_b)
    early_b = swap(pair_b, "dp", 1)
    out_a = call(
        functools.partial(chunk_kernel, share, chunk_a, chunk_a, 1, 7),
        shared + terms_a,
        (block_a, first_a, second_a, third_a, across_a) + weights + tuple(own_out[:7]),
        SMALL,
        16,
        aliases={8 + j: j for j in range(7)},
    )
    both_b, early_b, *out_a = fence(both_b, early_b, *out_a)

    partial = call(
        functools.partial(early_kernel, share),
        [shape(capacity, hidden_part, dtype=F32)] * 3,
        (pair_b, both_b, early_b) + weights,
        SMALL,
        16,
    )
    later_b = swap(both_b, "dp", 1)
    other_a = swap(out_a[6], "dp", 1)
    later_b, other_a, *out_a = fence(later_b, other_a, *out_a, *partial)
    out_a, partial = out_a[:7], tuple(out_a[7:])
    out_b = call(
        functools.partial(late_kernel, share, chunk_b),
        shared + terms_b[:1],
        (pair_b, both_b, early_b, later_b)
        + partial
        + weights
        + tuple(out_a[:5]),
        SMALL,
        16,
        aliases={10 + j: j for j in range(5)},
    )
    out_b = fence(*out_b)
    x_all, y_all, hidden, gate_grad, up_grad, odd_b = out_b
    (even_b,) = call(
        functools.partial(even_kernel, share, chunk_b),
        terms_b[:1],
        (gate_grad, up_grad) + weights[:2],
        SMALL,
        16,
    )
    other_b, even_b = fence(swap(odd_b, "dp", 1), even_b)

    def wgrad(left, right):
        blocks = 4
        scratch = [
            pltpu.VMEM((blocks, left.shape[1] // blocks, right.shape[1]), BF16),
            pltpu.SemaphoreType.DMA((blocks,)),
        ]
        (out,) = call(
            wgrad_kernel,
            [shape(left.shape[1], right.shape[1])],
            (left, right),
            SMALL,
            16,
            scratch,
            out_space=HBM,
        )
        return out

    pairs_a = core_pairs(out_a[5], other_a)
    pairs_b = core_pairs(even_b, other_b)
    pairs = [jnp.concatenate([pairs_a[j], pairs_b[j]]) for j in range(4)]
    relay = swap_second(pairs[3])
    late = swap_second(pairs[2])
    (relay,) = fence(relay)
    half = 2 * capacity
    step = total_of([pairs[1], relay])
    last_a = swap_first(step[:half])
    last_b = swap_first(step[half:])
    up_wgrad = wgrad(x_all, up_grad)
    last_a, late, up_wgrad, x_all = fence(last_a, late, up_wgrad, x_all)
    summed_a = total_of([pairs[0][:half], last_a, late[:half]])
    ret3 = swap(summed_a[capacity:], "expert", 3)
    ret1 = swap(summed_a[:capacity], "expert", 1)
    summed_a, last_b = fence(summed_a, last_b)
    summed_b = total_of([pairs[0][half:], last_b, late[half:]])
    ret0 = summed_b[:capacity]
    ret2 = swap(summed_b[capacity:], "expert", 2)
    gate_wgrad = wgrad(x_all, gate_grad)
    ret1, ret2, ret3, gate_wgrad = fence(ret1, ret2, ret3, gate_wgrad)
    (token_cols,) = call(
        combine_kernel,
        [shape(count, share)],
        (assign, ret0, ret1, ret2, ret3),
        SMALL,
        8,
        [pltpu.VMEM((experts * capacity, share), BF16)],
    )
    sixth = swap(token_cols, "dp", 6)
    first = swap_first(token_cols)
    second = swap_second(token_cols)
    down_wgrad = wgrad(hidden, y_all)
    first, second, sixth, down_wgrad = fence(first, second, sixth, down_wgrad)
    across = swap(jnp.concatenate([token_cols, first, second, sixth]), "dp", 1)
    (placed,) = call(
        functools.partial(place_kernel, share, 0, 4),
        [shape(count, width)],
        (token_cols, first, second, sixth),
        SMALL,
        8,
        [pltpu.SemaphoreType.DMA((4,))],
        out_space=HBM,
    )
    across, placed = fence(across, placed)
    (grad_tokens,) = pl.pallas_call(
        functools.partial(place_kernel, share, 1, 1),
        out_shape=[shape(count, width)],
        in_specs=[pl.BlockSpec(memory_space=VMEM), pl.BlockSpec(memory_space=HBM)],
        out_specs=[pl.BlockSpec(memory_space=HBM)],
        scratch_shapes=[pltpu.SemaphoreType.DMA((4,))],
        input_output_aliases={1: 0},
        compiler_params=pltpu.CompilerParams(vmem_limit_bytes=8 << 20),
    )(across, pltpu.with_memory_space_constraint(placed, HBM))
    return (grad_tokens, gate_wgrad[None], up_wgrad[None], down_wgrad[None])


def solution(mesh):
    placed = (
        P("expert", None),
        P("expert", None),
        P("expert", None),
        P("expert", None),
        P("expert", None, "dp"),
        P("expert", None, "dp"),
        P("expert", "dp", None),
    )
    fits = mesh.shape["dp"] == 8 and mesh.shape["expert"] == 4
    return jax.shard_map(
        per_device_blocks if fits else per_device_any,
        mesh=mesh,
        in_specs=placed,
        out_specs=(
            P("expert", None),
            P("expert", None, "dp"),
            P("expert", None, "dp"),
            P("expert", "dp", None),
        ),
        check_vma=False,
    )
```
